32 devices in a mesh: seq: 8 (over z, y), tp: 4 (over x, core).
Axes of the slice: x: 2, y: 2, z: 4, core: 2. Of those that a mesh axis runs over, the one named last changes fastest.
Arguments:
- inputs: bfloat16 [16, 1024, 768], P(None, 'seq'), may hold values from -6 to 6
- lengths: int32 [16], replicated, may hold values from 256 to 1024, as said below
- first_gain: float32 [768], replicated, may hold values from 0.5 to 1.5
- query_weight: bfloat16 [768, 768], P(None, 'tp'), may hold values from -0.21875 to 0.21875
- key_weight: bfloat16 [768, 768], P(None, 'tp'), may hold values from -0.21875 to 0.21875
- value_weight: bfloat16 [768, 768], P(None, 'tp'), may hold values from -0.21875 to 0.21875
- shift_taps: float32 [4, 768], P(None, 'tp'), may hold values from -3 to 3
- state_coef: float32 [768, 64], P('tp'), may hold values from -0.1875 to 0.1875
- state_rate: float32 [768, 64], P('tp'), may hold values from 0.00048828125 to 0.2
- skip_gain: float32 [768], P('tp'), may hold values from -3 to 3
- project_weight: bfloat16 [768, 768], P('tp'), may hold values from -0.21875 to 0.21875
- second_gain: float32 [768], replicated, may hold values from 0.5 to 1.5
- up_weight: bfloat16 [768, 3072], P(None, 'tp'), may hold values from -0.21875 to 0.21875
- down_weight: bfloat16 [3072, 768], P('tp'), may hold values from -0.109375 to 0.109375
- cotangent: bfloat16 [16, 1024, 768], P(None, 'seq'), may hold values from -6 to 6
Outputs:
- block_out: float32 [16, 1024, 768], P(None, 'seq')
- grad_inputs: float32 [16, 1024, 768], P(None, 'seq')
- grad_first: float32 [768], replicated
- grad_query: float32 [768, 768], P(None, 'tp')
- grad_key: float32 [768, 768], P(None, 'tp')
- grad_value: float32 [768, 768], P(None, 'tp')
- grad_taps: float32 [4, 768], P(None, 'tp')
- grad_coef: float32 [768, 64], P('tp')
- grad_rate: float32 [768, 64], P('tp')
- grad_skip: float32 [768], P('tp')
- grad_project: float32 [768, 768], P('tp')
- grad_second: float32 [768], replicated
- grad_up: float32 [768, 3072], P(None, 'tp')
- grad_down: float32 [3072, 768], P('tp')
The draws below stay inside these ranges and needn't reach their ends.
Inputs may be any that keep to these rules, and one draw needn't show every extreme that they name: `lengths`: one of the 16 sequences, which one drawn from the seed, has exactly 1024 tokens; positions from a sequence's length on are padding.
All inputs are finite; a program needn't handle non-finite values.
Results may differ from the reference program's by a relative error of at most 0.0075.
Values sent between devices are 32-bit elements; how exact they have to be, the bound alone decides.
No kernel may reach another device: no remote copies, remote signals or barrier semaphores. Data moves between devices by JAX's collectives and lax.ppermute only.
A program may use at most 192 MiB of HBM per device.

```python
import math
import jax
import jax.numpy as jnp
from jax import lax

D = 768
FF = 3072
STATE = 64
WIDTH = 4
BATCH = 16
MINLEN = 256
SEQLEN = 1024


def draw_lengths(key, part):
    first_key, second_key = jax.random.split(key)
    drawn = jax.random.randint(first_key, (BATCH,), MINLEN, SEQLEN + 1)
    chosen = jax.random.randint(second_key, (), 0, BATCH)
    return jnp.where(jnp.arange(BATCH) == chosen, SEQLEN, drawn).astype(jnp.int32)


def block_levels(key, shape, pieces, low, high):
    def one(axis_at, blocks):
        draws = jax.random.uniform(jax.random.fold_in(jax.random.fold_in(key, 6), axis_at), (blocks,), jnp.float32, low / len(pieces), high / len(pieces))
        return jnp.repeat(jnp.exp(draws), shape[axis_at] // blocks).reshape((-1,) + (1,) * (len(shape) - axis_at - 1))

    level = one(*pieces[0])
    for cut in pieces[1:]:
        level = level * one(*cut)
    return level


def bell_draw(rng, shape, width, most, pieces=(), dtype=jnp.bfloat16):
    values = width * jax.random.normal(rng, shape, jnp.float32)
    if pieces:
        values = values * block_levels(rng, shape, pieces, -0.22, 0.18)
    return jnp.clip(values, -most, most).astype(dtype)


def setup_inputs(seed: int = 0) -> dict:
    splits = jax.random.split(jax.random.key(seed), 16)
    inputs = bell_draw(splits[0], (BATCH, SEQLEN, D), 1.0, 6.0, ((1, 8),))
    lengths = draw_lengths(jax.random.fold_in(splits[15], 71), 0)
    first_gain = jnp.clip(1.0 + 0.1 * jax.random.normal(splits[2], (D,), jnp.float32), 0.5, 1.5)
    query_weight = bell_draw(splits[3], (D, D), D ** -0.5, 0.21875, ((1, 4),))
    key_weight = bell_draw(splits[4], (D, D), D ** -0.5, 0.21875, ((1, 4),))
    value_weight = bell_draw(splits[5], (D, D), D ** -0.5, 0.21875, ((1, 4),))
    shift_taps = bell_draw(splits[6], (WIDTH, D), WIDTH ** -0.5, 3.0, ((1, 4),), jnp.float32)
    state_coef = bell_draw(splits[7], (D, STATE), (0.4 / SEQLEN ** 0.5), 0.1875, ((0, 4),), jnp.float32)
    state_rate = jnp.clip(jnp.exp(math.log(0.2) - 6.015181 * jax.random.uniform(splits[8], (D, STATE), jnp.float32) ** block_levels(splits[8], (D, STATE), ((0, 4),), -0.2, 0.2)), 0.00048828125, 0.2)
    skip_gain = bell_draw(splits[9], (D,), 1.0, 3.0, ((0, 4),), jnp.float32)
    project_weight = bell_draw(splits[10], (D, D), D ** -0.5, 0.21875, ((0, 4),))
    second_gain = jnp.clip(1.0 + 0.1 * jax.random.normal(splits[11], (D,), jnp.float32), 0.5, 1.5)
    up_weight = bell_draw(splits[12], (D, FF), D ** -0.5, 0.21875, ((1, 4),))
    down_weight = bell_draw(splits[13], (FF, D), FF ** -0.5, 0.109375, ((0, 4),))
    cotangent = bell_draw(splits[14], (BATCH, SEQLEN, D), 1.0, 6.0, ((1, 8),))
    return dict(inputs=inputs, lengths=lengths, first_gain=first_gain, query_weight=query_weight, key_weight=key_weight, value_weight=value_weight, shift_taps=shift_taps, state_coef=state_coef, state_rate=state_rate, skip_gain=skip_gain, project_weight=project_weight, second_gain=second_gain, up_weight=up_weight, down_weight=down_weight, cotangent=cotangent)


@jax.custom_vjp
def low(v):
    return lax.optimization_barrier(v.astype(jnp.bfloat16)).astype(jnp.float32)

@jax.custom_vjp
def low_back(v):
    return v

def low_keep(v):
    return (low(v), None)

def low_pass(kept, grad):
    return (grad,)

def back_keep(v):
    return (v, None)

def back_low(kept, grad):
    return (low(grad),)
low.defvjp(low_keep, low_pass)
low_back.defvjp(back_keep, back_low)

def layer_norm(rows, gain):
    center = rows - lax.optimization_barrier(jnp.mean(rows, axis=-1, keepdims=True))
    spread = lax.optimization_barrier(jnp.mean(center * center, axis=-1, keepdims=True))
    return center * lax.rsqrt(spread + 1e-05) * gain

def kernel_values(coef, rate, freq, parity, total, length):
    half = jnp.pi * freq / total
    below = jnp.sin(half)
    square = (below * below)[:, None, None]
    whole = jnp.sin(2.0 * half)[:, None, None]
    decay = jnp.exp(-rate)
    gap = -jnp.expm1(-rate)
    ending = jnp.exp(-rate * length)
    numer = 1.0 - parity[:, None, None] * ending
    denom = gap * gap + 4.0 * decay * square
    real_term = numer * (gap + 2.0 * decay * square) / denom
    imag_term = -numer * decay * whole / denom
    return (lax.optimization_barrier(jnp.sum(coef * real_term, axis=-1)), lax.optimization_barrier(jnp.sum(coef * imag_term, axis=-1)))

def full_kernel(state_coef, state_rate):
    total = 2 * SEQLEN
    index = jnp.arange(total)
    freq = index.astype(jnp.float32)
    parity = (1 - 2 * (index % 2)).astype(jnp.float32)
    blocks = D // 16

    def one_block(pair):
        return kernel_values(pair[0], pair[1], freq, parity, total, SEQLEN)
    real_part, imag_part = lax.map(jax.checkpoint(one_block), (state_coef.reshape(blocks, 16, STATE), state_rate.reshape(blocks, 16, STATE)))
    real_part = jnp.transpose(real_part, (1, 0, 2)).reshape(total, D)
    imag_part = jnp.transpose(imag_part, (1, 0, 2)).reshape(total, D)
    return (real_part, imag_part)

def matmul(left, right, form):
    return jnp.einsum(form, left, right, precision=lax.Precision.HIGHEST)

def reference(inputs, lengths, first_gain, query_weight, key_weight, value_weight, shift_taps, state_coef, state_rate, skip_gain, project_weight, second_gain, up_weight, down_weight, cotangent):
    validity = (jnp.arange(SEQLEN)[None, :] < lengths[:, None]).astype(jnp.float32)[:, :, None]

    def forward(source, gain_a, w_query, w_key, w_value, taps, coef, rate, skip, w_project, gain_b, w_up, w_down):
        normed = low(layer_norm(source, gain_a))
        queries = low_back(matmul(normed, w_query, 'btd,de->bte'))
        key_rows = low_back(matmul(normed, w_key, 'btd,de->bte'))
        values = low_back(matmul(normed, w_value, 'btd,de->bte'))
        padded = jnp.pad(key_rows, ((0, 0), (WIDTH - 1, 0), (0, 0)))
        shifted = jnp.zeros_like(key_rows)
        for offset in range(WIDTH):
            shifted = shifted + taps[offset] * padded[:, WIDTH - 1 - offset:WIDTH - 1 - offset + SEQLEN, :]
        mixed_in = shifted * values
        kernel_re, kernel_im = full_kernel(coef, rate)
        kernel = lax.complex(kernel_re, kernel_im)
        spectrum = jnp.fft.fft(jnp.pad(mixed_in, ((0, 0), (0, SEQLEN), (0, 0))), axis=1)
        conv = jnp.real(jnp.fft.ifft(spectrum * kernel[None], axis=1))[:, :SEQLEN, :]
        state_out = conv + skip * mixed_in
        gated_out = low(queries * state_out)
        residual = source + low_back(matmul(gated_out, w_project, 'btc,cd->btd'))
        second = low(layer_norm(residual, gain_b))
        up_act = low_back(matmul(second, w_up, 'btd,df->btf'))
        hidden = low(jax.nn.gelu(up_act))
        return validity * (residual + matmul(hidden, w_down, 'btf,fd->btd'))
    primal = (inputs.astype(jnp.float32), first_gain, query_weight.astype(jnp.float32), key_weight.astype(jnp.float32), value_weight.astype(jnp.float32), shift_taps, state_coef, state_rate, skip_gain, project_weight.astype(jnp.float32), second_gain, up_weight.astype(jnp.float32), down_weight.astype(jnp.float32))
    block_out, pullback = jax.vjp(forward, *primal)
    grads = pullback(cotangent.astype(jnp.float32))
    return (block_out, grads[0], grads[1], grads[2], grads[3], grads[4], grads[5], grads[6], grads[7], grads[8], grads[9], grads[10], grads[11], grads[12])
```

```python
import jax
import jax.numpy as jnp
from jax import lax
from jax.experimental import pallas as pl
from jax.experimental.pallas import tpu as pltpu
from jax.sharding import PartitionSpec as P

LANES = 128
GROUP = 16
BF = jnp.bfloat16
F32 = jnp.float32


def iota2(axis):
    return lax.broadcasted_iota(jnp.int32, (LANES, LANES), axis)


def strided(ref, c, rows):
    return ref[pl.ds(c, rows, stride=GROUP), :]


def lag_rows(block, edge, offset, lane):
    return pltpu.roll(jnp.where(lane < LANES - offset, block, edge), offset, 1)


def unpack_tail(tail, b, taps):
    return pltpu.roll(tail, (LANES - (taps - 1) * (b + 1)) % LANES, 1)


def shift_sum(block, tail, b, taps_ref, taps, lane):
    edge = unpack_tail(tail, b, taps)
    total = taps_ref[:, 0:1] * block
    for offset in range(1, taps):
        total = total + taps_ref[:, offset : offset + 1] * lag_rows(block, edge, offset, lane)
    return total


def fwd_local_kernel(
    k_ref, v_ref, tail_ref, taps_ref, rate_ref, kern_ref, y_ref, h_ref, h1_ref, mix_ref, out_ref
):
    batch = k_ref.shape[0]
    taps = taps_ref.shape[1]
    lane = lax.broadcasted_iota(jnp.int32, (GROUP, LANES), 1)
    tail = tail_ref[...]
    for b in range(batch):
        mixed = shift_sum(k_ref[b], tail, b, taps_ref, taps, lane) * v_ref[b]
        mix_ref[b * GROUP : (b + 1) * GROUP, :] = mixed
    row = iota2(0)
    col = iota2(1)
    away = (LANES - 1 - row).astype(F32)
    low_half = lax.broadcasted_iota(jnp.int32, (batch, LANES), 1) < LANES // 2
    for p in range(GROUP // 2):
        xs = []
        for c in (2 * p, 2 * p + 1):
            x = strided(mix_ref, c, batch).astype(BF)
            xs.append(x)
            spread = jnp.broadcast_to(kern_ref[c : c + 1, :], (LANES, LANES))
            toep = pltpu.roll(spread, 0, 1, stride=1, stride_axis=0)
            toep = jnp.where(col >= row, toep, 0.0).astype(BF)
            out_ref[pl.ds(c, batch, stride=GROUP), :] = jnp.dot(
                x, toep, preferred_element_type=F32
            )
        decay = jnp.exp(-rate_ref[p : p + 1, :] * away)
        both = jnp.concatenate(xs, axis=0)
        grown = jnp.dot(both, decay.astype(BF), preferred_element_type=F32)
        h_ref[p] = jnp.where(low_half, grown[:batch], grown[batch:])
        grown = jnp.dot(both, (decay * away).astype(BF), preferred_element_type=F32)
        h1_ref[p] = jnp.where(low_half, grown[:batch], grown[batch:])
    for b in range(batch):
        y_ref[b] = out_ref[b * GROUP : (b + 1) * GROUP, :]


def fwd_post_kernel(
    y_ref, hin_ref, coef_ref, rate_ref, k_ref, v_ref, tail_ref, taps_ref, q_ref, skip_ref,
    state_ref, gated_ref, out_ref,
):
    batch = k_ref.shape[0]
    taps = taps_ref.shape[1]
    ahead = (iota2(0) + 1).astype(F32)
    low_half = lax.broadcasted_iota(jnp.int32, (batch, LANES), 1) < LANES // 2
    for p in range(GROUP // 2):
        grow = jnp.exp(-rate_ref[p : p + 1, :] * ahead).astype(BF)
        h = hin_ref[p] * coef_ref[p : p + 1, :]
        both = jnp.concatenate([jnp.where(low_half, h, 0.0), jnp.where(low_half, 0.0, h)], axis=0)
        cross = lax.dot_general(
            both.astype(BF), grow, (((1,), (1,)), ((), ())), preferred_element_type=F32
        )
        out_ref[pl.ds(2 * p, batch, stride=GROUP), :] = cross[:batch]
        out_ref[pl.ds(2 * p + 1, batch, stride=GROUP), :] = cross[batch:]
    lane = lax.broadcasted_iota(jnp.int32, (GROUP, LANES), 1)
    tail = tail_ref[...]
    for b in range(batch):
        mixed = shift_sum(k_ref[b], tail, b, taps_ref, taps, lane) * v_ref[b]
        state = y_ref[b] + out_ref[b * GROUP : (b + 1) * GROUP, :] + skip_ref[...] * mixed
        state_ref[b] = state
        gated_ref[b] = (q_ref[b] * state).astype(BF)


def bwd_local_kernel(
    dg_ref, q_ref, state_ref, k_ref, v_ref, tail_ref, taps_ref, skip_ref, rate_ref, kern_ref,
    dq_ref, dx_ref, g_ref, g1_ref, lag_ref, s0_ref, s1_ref, x_scr, d_scr, out_ref,
):
    batch = k_ref.shape[0]
    taps = taps_ref.shape[1]
    lane = lax.broadcasted_iota(jnp.int32, (GROUP, LANES), 1)
    tail = tail_ref[...]
    for b in range(batch):
        x_scr[b * GROUP : (b + 1) * GROUP, :] = (
            shift_sum(k_ref[b], tail, b, taps_ref, taps, lane) * v_ref[b]
        )
        dg = dg_ref[b]
        dq_ref[b] = (dg * state_ref[b]).astype(BF)
        d_scr[b * GROUP : (b + 1) * GROUP, :] = dg * q_ref[b]
    row = iota2(0)
    col = iota2(1)
    mirror = jnp.where(row + col == LANES - 1, 1.0, 0.0).astype(BF)
    ahead = (row + 1).astype(F32)
    low_half = lax.broadcasted_iota(jnp.int32, (batch, LANES), 1) < LANES // 2
    low_row = lax.broadcasted_iota(jnp.int32, (1, LANES), 1) < LANES // 2
    for p in range(GROUP // 2):
        ds = []
        lags = []
        for c in (2 * p, 2 * p + 1):
            x = strided(x_scr, c, batch).astype(BF)
            d = strided(d_scr, c, batch).astype(BF)
            ds.append(d)
            spread = jnp.broadcast_to(kern_ref[c : c + 1, :], (LANES, LANES))
            toep = pltpu.roll(spread, 0, 1, stride=1, stride_axis=0)
            toep = jnp.where(col >= row, toep, 0.0).astype(BF)
            out_ref[pl.ds(c, batch, stride=GROUP), :] = lax.dot_general(
                d, toep, (((1,), (1,)), ((), ())), preferred_element_type=F32
            )
            x = jnp.dot(x, mirror, preferred_element_type=F32).astype(BF)
            pairs = lax.dot_general(x, d, (((0,), (0,)), ((), ())), preferred_element_type=F32)
            pairs = jnp.where(col + row >= LANES - 1, pairs, 0.0)
            pairs = pltpu.roll(pairs, 1, 1, stride=1, stride_axis=0)
            lag = jnp.sum(pairs, axis=0, keepdims=True)
            lag_ref[c : c + 1, :] = lag
            lags.append(lag)
        grow = jnp.exp(-rate_ref[p : p + 1, :] * ahead)
        grow_low = grow.astype(BF)
        grow1_low = (grow * ahead).astype(BF)
        both = jnp.concatenate(ds, axis=0)
        got = jnp.dot(both, grow_low, preferred_element_type=F32)
        g_ref[p] = jnp.where(low_half, got[:batch], got[batch:])
        got = jnp.dot(both, grow1_low, preferred_element_type=F32)
        g1_ref[p] = jnp.where(low_half, got[:batch], got[batch:])
        high = [lag.astype(BF).astype(F32) for lag in lags]
        lagrow = lax.broadcasted_iota(jnp.int32, (8, LANES), 0)
        stack = jnp.where(
            lagrow == 0, high[0], jnp.where(lagrow == 1, high[1],
            jnp.where(lagrow == 2, lags[0] - high[0], jnp.where(lagrow == 3, lags[1] - high[1], 0.0)))
        ).astype(BF)
        got = jnp.dot(stack, grow_low, preferred_element_type=F32)
        s0_ref[p : p + 1, :] = jnp.where(low_row, got[0:1] + got[2:3], got[1:2] + got[3:4])
        got = jnp.dot(stack, grow1_low, preferred_element_type=F32)
        s1_ref[p : p + 1, :] = jnp.where(low_row, got[0:1] + got[2:3], got[1:2] + got[3:4])
    for b in range(batch):
        sl = slice(b * GROUP, (b + 1) * GROUP)
        dx_ref[b] = out_ref[sl, :] + skip_ref[...] * d_scr[sl, :]


def bwd_post_kernel(
    dx_ref, gin_ref, coef_ref, rate_ref, k_ref, v_ref, tail_ref, taps_ref,
    dv_ref, ds_ref, head_ref, gtap_ref, out_ref,
):
    batch = k_ref.shape[0]
    taps = taps_ref.shape[1]
    away = (LANES - 1 - iota2(0)).astype(F32)
    low_half = lax.broadcasted_iota(jnp.int32, (batch, LANES), 1) < LANES // 2
    for p in range(GROUP // 2):
        decay = jnp.exp(-rate_ref[p : p + 1, :] * away).astype(BF)
        g = gin_ref[p] * coef_ref[p : p + 1, :]
        both = jnp.concatenate([jnp.where(low_half, g, 0.0), jnp.where(low_half, 0.0, g)], axis=0)
        cross = lax.dot_general(
            both.astype(BF), decay, (((1,), (1,)), ((), ())), preferred_element_type=F32
        )
        out_ref[pl.ds(2 * p, batch, stride=GROUP), :] = cross[:batch]
        out_ref[pl.ds(2 * p + 1, batch, stride=GROUP), :] = cross[batch:]
    lane = lax.broadcasted_iota(jnp.int32, (GROUP, LANES), 1)
    tail = tail_ref[...]
    head = jnp.zeros((GROUP, LANES), F32)
    sums = [jnp.zeros((GROUP, LANES), F32) for _ in range(taps)]
    for b in range(batch):
        block = k_ref[b]
        edge = unpack_tail(tail, b, taps)
        lagged = [block] + [lag_rows(block, edge, i, lane) for i in range(1, taps)]
        shifted = taps_ref[:, 0:1] * block
        for i in range(1, taps):
            shifted = shifted + taps_ref[:, i : i + 1] * lagged[i]
        d_mixed = dx_ref[b] + out_ref[b * GROUP : (b + 1) * GROUP, :]
        dv_ref[b] = (d_mixed * shifted).astype(BF)
        d_shifted = d_mixed * v_ref[b]
        ds_ref[b] = d_shifted
        for i in range(taps):
            sums[i] = sums[i] + d_shifted * lagged[i]
        start = (taps - 1) * b
        head = jnp.where(
            (lane >= start) & (lane < start + taps - 1), pltpu.roll(d_shifted, start, 1), head
        )
    head_ref[...] = head
    packed = jnp.zeros((GROUP, LANES), F32)
    for i in range(taps):
        packed = jnp.where(lane == i, jnp.sum(sums[i], axis=1, keepdims=True), packed)
    gtap_ref[...] = packed


def specs(batch, taps):
    return dict(
        act=pl.BlockSpec((batch, GROUP, LANES), lambda i: (0, i, 0)),
        row=pl.BlockSpec((GROUP, LANES), lambda i: (i, 0)),
        pair=pl.BlockSpec((GROUP // 2, LANES), lambda i: (i, 0)),
        state=pl.BlockSpec((GROUP // 2, batch, LANES), lambda i: (i, 0, 0)),
        taps=pl.BlockSpec((GROUP, taps), lambda i: (i, 0)),
        one=pl.BlockSpec((GROUP, 1), lambda i: (i, 0)),
    )


def shape(*dims, dtype=F32):
    return jax.ShapeDtypeStruct(dims, dtype)


def call(kernel, ins, outs, out_shapes, scratch, channels, args):
    return pl.pallas_call(
        kernel,
        grid=(channels // GROUP,),
        in_specs=ins,
        out_specs=outs,
        out_shape=out_shapes,
        scratch_shapes=scratch,
    )(*args)


def conv_calls(batch, channels, taps):
    s = specs(batch, taps)
    act, row, pair, state, tap, one = (s[n] for n in ("act", "row", "pair", "state", "taps", "one"))
    a = shape(batch, channels, LANES)
    alow = shape(batch, channels, LANES, dtype=BF)
    st = shape(channels // 2, batch, LANES)
    rows = shape(channels, LANES)
    pairs = shape(channels // 2, LANES)
    scr = pltpu.VMEM((batch * GROUP, LANES), F32)

    def fwd_local(k, v, tail, tap_rows, rate, kern):
        return call(fwd_local_kernel, [act, act, row, tap, pair, row], [act, state, state],
                    [a, st, st], [scr, scr], channels, (k, v, tail, tap_rows, rate, kern))

    def fwd_post(y, hin, coef, rate, k, v, tail, tap_rows, q, skip):
        return call(fwd_post_kernel, [act, state, pair, pair, act, act, row, tap, act, one],
                    [act, act], [a, alow], [scr], channels,
                    (y, hin, coef, rate, k, v, tail, tap_rows, q, skip))

    def bwd_local(dg, q, so, k, v, tail, tap_rows, skip, rate, kern):
        return call(bwd_local_kernel, [act, act, act, act, act, row, tap, one, pair, row],
                    [act, act, state, state, row, pair, pair], [alow, a, st, st, rows, pairs, pairs],
                    [scr, scr, scr], channels, (dg, q, so, k, v, tail, tap_rows, skip, rate, kern))

    def bwd_post(dx, gin, coef, rate, k, v, tail, tap_rows):
        return call(bwd_post_kernel, [act, state, pair, pair, act, act, row, tap],
                    [act, act, row, row], [alow, a, rows, rows], [scr], channels,
                    (dx, gin, coef, rate, k, v, tail, tap_rows))

    return fwd_local, fwd_post, bwd_local, bwd_post


def passed_along(x, axis, by):
    count = lax.axis_size(axis)
    pairs = [(i, i + by) for i in range(count) if 0 <= i + by < count]
    return lax.ppermute(x, axis, pairs)


def carried(own, decay, sign):
    count = lax.axis_size("seq")
    got = passed_along(own, "seq", sign)
    reach = 1
    while reach < count - 1:
        whole = own + decay(1) * got
        got = got + decay(reach) * passed_along(whole, "seq", sign * (reach + 1))
        reach = 2 * reach + 1
    return got


def layer_norm(rows, gain):
    center = rows - jnp.mean(rows, axis=-1, keepdims=True)
    spread = jnp.mean(center * center, axis=-1, keepdims=True)
    return center * lax.rsqrt(spread + 1e-05) * gain


def product(form, left, right):
    return jnp.einsum(form, left, right, preferred_element_type=F32)


def pack_edges(rows, lanes):
    num_seqs, channels, count = rows.shape
    flat = jnp.transpose(rows, (1, 0, 2)).reshape(channels, num_seqs * count)
    return jnp.pad(flat, ((0, 0), (0, lanes - num_seqs * count)))


def local(
    inputs,
    lengths,
    first_gain,
    query_weight,
    key_weight,
    value_weight,
    shift_taps,
    state_coef,
    state_rate,
    skip_gain,
    project_weight,
    second_gain,
    up_weight,
    down_weight,
    cotangent,
):
    num_dev = lax.axis_size("seq")
    place = lax.axis_index("seq")
    num_seqs, block_len, width_all = inputs.shape
    taps = shift_taps.shape[0]
    channels, states = state_coef.shape
    assert block_len == LANES and 2 * states == LANES and channels % GROUP == 0
    edge = taps - 1
    source = inputs.astype(F32)
    positions = place * block_len + jnp.arange(block_len)
    validity = (positions[None, :] < lengths[:, None]).astype(F32)[:, :, None]
    fwd_local, fwd_post, bwd_local, bwd_post = conv_calls(num_seqs, channels, taps)
    rate = state_rate.reshape(channels // 2, LANES)
    coef = state_coef.reshape(channels // 2, LANES)
    tap_rows = shift_taps.T
    skip = skip_gain[:, None]
    lag = jnp.arange(LANES).astype(F32)
    kern = jnp.sum(
        state_coef[:, :, None] * jnp.exp(-state_rate[:, :, None] * lag[None, None, :]), axis=1
    )

    def block_decay(count):
        return jnp.exp(-rate * (LANES * count))[:, None, :]

    normed = layer_norm(source, first_gain).astype(BF)
    queries = product("btd,dc->bct", normed, query_weight)
    keys = product("btd,dc->bct", normed, key_weight)
    values = product("btd,dc->bct", normed, value_weight)
    tail = passed_along(pack_edges(keys[:, :, block_len - edge :], LANES), "seq", 1)
    conv, own, own_lag = fwd_local(keys, values, tail, tap_rows, rate, kern)
    before = carried(own, block_decay, 1)
    state_out, gated_out = fwd_post(
        conv, before, coef, rate, keys, values, tail, tap_rows, queries, skip
    )
    mixer = lax.psum(product("bct,cd->btd", gated_out, project_weight), "tp")
    residual = source + mixer
    second = layer_norm(residual, second_gain).astype(BF)
    up_act = product("btd,df->btf", second, up_weight)
    hidden = jax.nn.gelu(up_act).astype(BF)
    lowered = lax.psum(product("btf,fd->btd", hidden, down_weight), "tp")
    block_out = validity * (residual + lowered)
    d_mlp = validity * cotangent.astype(F32)
    d_mlp_low = d_mlp.astype(BF)
    grad_down = product("btf,btd->fd", hidden, d_mlp_low)
    d_hidden = product("btd,fd->btf", d_mlp_low, down_weight)
    gelu_value, gelu_pull = jax.vjp(jax.nn.gelu, up_act)
    d_up = gelu_pull(d_hidden)[0].astype(BF)
    grad_up = product("btd,btf->df", second, d_up)
    d_second = lax.psum(product("btf,df->btd", d_up, up_weight), "tp")
    norm_value, second_pull = jax.vjp(layer_norm, residual, second_gain)
    d_resid_norm, grad_second = second_pull(d_second)
    d_residual = d_mlp + d_resid_norm
    d_resid_low = d_residual.astype(BF)
    grad_project = product("bct,btd->cd", gated_out, d_resid_low)
    d_gated = product("btd,cd->bct", d_resid_low, project_weight)
    d_queries, d_part, back, back_lag, lags, near, near_lag = bwd_local(
        d_gated, queries, state_out, keys, values, tail, tap_rows, skip, rate, kern
    )
    after = carried(back, block_decay, -1)
    d_values, d_shifted, head, grad_taps = bwd_post(
        d_part, after, coef, rate, keys, values, tail, tap_rows
    )
    grow = jnp.exp(rate)
    grad_coef = jnp.sum(before * back, axis=1) + grow * near
    grad_rate = -coef * (
        jnp.sum(
            back_lag * before + after * (own_lag + LANES * block_decay(1) * before), axis=1
        )
        + grow * (near_lag - near)
    )
    grad_coef = grad_coef.reshape(channels, states)
    grad_rate = grad_rate.reshape(channels, states)
    grad_skip = lags[:, 0]
    grad_taps = grad_taps[:, :taps].T
    spill = passed_along(head, "seq", -1)
    spill = spill[:, : num_seqs * edge].reshape(channels, num_seqs, edge)
    ahead = jnp.concatenate([d_shifted, jnp.transpose(spill, (1, 0, 2))], axis=2)
    d_keys = sum(
        tap_rows[:, i][None, :, None] * ahead[:, :, i : i + block_len] for i in range(taps)
    ).astype(BF)
    grad_query = product("btd,bct->dc", normed, d_queries)
    grad_key = product("btd,bct->dc", normed, d_keys)
    grad_value = product("btd,bct->dc", normed, d_values)
    d_first_part = product("bct,dc->btd", d_queries, query_weight)
    d_first_part = d_first_part + product("bct,dc->btd", d_keys, key_weight)
    d_first_part = d_first_part + product("bct,dc->btd", d_values, value_weight)
    d_first = lax.psum(d_first_part, "tp")
    first_value, first_pull = jax.vjp(layer_norm, source, first_gain)
    d_input_norm, grad_first = first_pull(d_first)
    grad_inputs = d_residual + d_input_norm
    grads = lax.psum(
        (
            grad_first,
            grad_query,
            grad_key,
            grad_value,
            grad_taps,
            grad_coef,
            grad_rate,
            grad_skip,
            grad_project,
            grad_second,
            grad_up,
            grad_down,
        ),
        "seq",
    )
    return (block_out, grad_inputs, *grads)


def solution(mesh):
    return jax.shard_map(
        local,
        mesh=mesh,
        in_specs=(
            P(None, "seq", None),
            P(),
            P(),
            P(None, "tp"),
            P(None, "tp"),
            P(None, "tp"),
            P(None, "tp"),
            P("tp", None),
            P("tp", None),
            P("tp"),
            P("tp", None),
            P(),
            P(None, "tp"),
            P("tp", None),
            P(None, "seq", None),
        ),
        out_specs=(
            P(None, "seq", None),
            P(None, "seq", None),
            P(),
            P(None, "tp"),
            P(None, "tp"),
            P(None, "tp"),
            P(None, "tp"),
            P("tp", None),
            P("tp", None),
            P("tp"),
            P("tp", None),
            P(),
            P(None, "tp"),
            P("tp", None),
        ),
        check_vma=False,
    )
```

```python
import functools

import jax
import jax.numpy as jnp
from jax import lax
from jax.experimental import pallas as pl
from jax.experimental.pallas import tpu as pltpu
from jax.sharding import PartitionSpec as P

LANES = 128
GROUP = 32
BF = jnp.bfloat16
F32 = jnp.float32


def iota2(axis):
    return lax.broadcasted_iota(jnp.int32, (LANES, LANES), axis)


def strided(ref, c, rows):
    return ref[pl.ds(c, rows, stride=GROUP), :]


def lag_rows(block, edge, offset, lane):
    return pltpu.roll(jnp.where(lane < LANES - offset, block, edge), offset, 1)


def unpack_tail(tail, b, taps):
    return pltpu.roll(tail, (LANES - (taps - 1) * (b + 1)) % LANES, 1)


def spread_taps(taps_ref):
    rows, taps = taps_ref.shape
    return [jnp.broadcast_to(taps_ref[:, i : i + 1], (rows, LANES)) for i in range(taps)]


def shift_sum(block, tail, b, spread, lane):
    edge = unpack_tail(tail, b, len(spread))
    total = spread[0] * block
    for offset in range(1, len(spread)):
        total = total + spread[offset] * lag_rows(block, edge, offset, lane)
    return total


def fwd_local_kernel(
    k_ref, v_ref, tail_ref, taps_ref, rate_ref, kern_ref, y_ref, mixed_ref, h_ref, mix_ref, out_ref
):
    batch = k_ref.shape[0]
    lane = lax.broadcasted_iota(jnp.int32, (GROUP, LANES), 1)
    tail = tail_ref[...]
    spread = spread_taps(taps_ref)
    for b in range(batch):
        mixed = shift_sum(k_ref[b], tail, b, spread, lane) * v_ref[b]
        mix_ref[b * GROUP : (b + 1) * GROUP, :] = mixed
        mixed_ref[b] = mixed
    row = iota2(0)
    col = iota2(1)
    away = (LANES - 1 - row).astype(F32)
    low_half = lax.broadcasted_iota(jnp.int32, (batch, LANES), 1) < LANES // 2
    for p in range(GROUP // 2):
        xs = []
        for c in (2 * p, 2 * p + 1):
            x = strided(mix_ref, c, batch).astype(BF)
            xs.append(x)
            toep = jnp.broadcast_to(kern_ref[c : c + 1, :], (LANES, LANES))
            toep = pltpu.roll(toep, 0, 1, stride=1, stride_axis=0)
            toep = jnp.where(col >= row, toep, 0.0).astype(BF)
            out_ref[pl.ds(c, batch, stride=GROUP), :] = jnp.dot(
                x, toep, preferred_element_type=F32
            )
        decay = jnp.exp(-rate_ref[p : p + 1, :] * away)
        both = jnp.concatenate(xs, axis=0)
        grown = jnp.dot(both, decay.astype(BF), preferred_element_type=F32)
        h_ref[p] = jnp.where(low_half, grown[:batch], grown[batch:])
    for b in range(batch):
        y_ref[b] = out_ref[b * GROUP : (b + 1) * GROUP, :]


def fwd_post_kernel(
    y_ref, hin_ref, coef_ref, rate_ref, mixed_ref, q_ref, skip_ref, state_ref, gated_ref, out_ref
):
    batch = y_ref.shape[0]
    ahead = (iota2(0) + 1).astype(F32)
    low_half = lax.broadcasted_iota(jnp.int32, (batch, LANES), 1) < LANES // 2
    for p in range(GROUP // 2):
        grow = jnp.exp(-rate_ref[p : p + 1, :] * ahead).astype(BF)
        h = hin_ref[p] * coef_ref[p : p + 1, :]
        both = jnp.concatenate([jnp.where(low_half, h, 0.0), jnp.where(low_half, 0.0, h)], axis=0)
        cross = lax.dot_general(
            both.astype(BF), grow, (((1,), (1,)), ((), ())), preferred_element_type=F32
        )
        out_ref[pl.ds(2 * p, batch, stride=GROUP), :] = cross[:batch]
        out_ref[pl.ds(2 * p + 1, batch, stride=GROUP), :] = cross[batch:]
    skip = jnp.broadcast_to(skip_ref[...], (GROUP, LANES))
    for b in range(batch):
        state = y_ref[b] + out_ref[b * GROUP : (b + 1) * GROUP, :] + skip * mixed_ref[b]
        state_ref[b] = state
        gated_ref[b] = (q_ref[b] * state).astype(BF)


def bwd_local_kernel(
    dg_ref, q_ref, state_ref, skip_ref, rate_ref, kern_ref, dq_ref, d_ref, dx_ref, g_ref,
    d_scr, out_ref,
):
    batch = dg_ref.shape[0]
    for b in range(batch):
        dg = dg_ref[b]
        dq_ref[b] = (dg * state_ref[b]).astype(BF)
        d = dg * q_ref[b]
        d_ref[b] = d
        d_scr[b * GROUP : (b + 1) * GROUP, :] = d
    row = iota2(0)
    col = iota2(1)
    ahead = (row + 1).astype(F32)
    low_half = lax.broadcasted_iota(jnp.int32, (batch, LANES), 1) < LANES // 2
    for p in range(GROUP // 2):
        ds = []
        for c in (2 * p, 2 * p + 1):
            d = strided(d_scr, c, batch).astype(BF)
            ds.append(d)
            toep = jnp.broadcast_to(kern_ref[c : c + 1, :], (LANES, LANES))
            toep = pltpu.roll(toep, 1, 1, stride=1, stride_axis=0)
            toep = jnp.where(col <= row, toep, 0.0).astype(BF)
            out_ref[pl.ds(c, batch, stride=GROUP), :] = jnp.dot(
                d, toep, preferred_element_type=F32
            )
        grow = jnp.exp(-rate_ref[p : p + 1, :] * ahead)
        got = jnp.dot(jnp.concatenate(ds, axis=0), grow.astype(BF), preferred_element_type=F32)
        g_ref[p] = jnp.where(low_half, got[:batch], got[batch:])
    skip = jnp.broadcast_to(skip_ref[...], (GROUP, LANES))
    for b in range(batch):
        dx_ref[b] = out_ref[b * GROUP : (b + 1) * GROUP, :] + skip * d_ref[b]


def bwd_lags_kernel(
    d_ref, mixed_ref, rate_ref, h1_ref, g1_ref, lag_ref, s0_ref, s1_ref, x_scr, d_scr, turn_scr,
    grow_scr,
):
    batch = d_ref.shape[0]
    for b in range(batch):
        x_scr[b * GROUP : (b + 1) * GROUP, :] = mixed_ref[b]
        d_scr[b * GROUP : (b + 1) * GROUP, :] = d_ref[b]
    row = iota2(0)
    col = iota2(1)
    mirror = jnp.where(row + col == LANES - 1, 1.0, 0.0).astype(BF)
    ahead = (row + 1).astype(F32)
    away = (LANES - 1 - row).astype(F32)
    low_half = lax.broadcasted_iota(jnp.int32, (batch, LANES), 1) < LANES // 2
    low_row = lax.broadcasted_iota(jnp.int32, (1, LANES), 1) < LANES // 2
    lagrow = lax.broadcasted_iota(jnp.int32, (8, LANES), 0)
    for p in range(GROUP // 2):
        xs = jnp.concatenate([strided(x_scr, 2 * p + i, batch) for i in (0, 1)], axis=0).astype(BF)
        turn_scr[p] = jnp.dot(xs, mirror, preferred_element_type=F32).T.astype(BF)
        fall = jnp.exp(-rate_ref[p : p + 1, :] * away) * away
        got = jnp.dot(xs, fall.astype(BF), preferred_element_type=F32)
        h1_ref[p] = jnp.where(low_half, got[:batch], got[batch:])
    for p in range(GROUP // 2):
        ds = jnp.concatenate([strided(d_scr, 2 * p + i, batch) for i in (0, 1)], axis=0).astype(BF)
        for i in (0, 1):
            part = slice(i * batch, (i + 1) * batch)
            pairs = jnp.dot(turn_scr[p, :, part], ds[part], preferred_element_type=F32)
            pairs = jnp.where(col + row >= LANES - 1, pairs, 0.0)
            pairs = pltpu.roll(pairs, 1, 1, stride=1, stride_axis=0)
            lag_ref[2 * p + i : 2 * p + i + 1, :] = jnp.sum(pairs, axis=0, keepdims=True)
        grow = jnp.exp(-rate_ref[p : p + 1, :] * ahead)
        grow_scr[p, :, :LANES] = grow.astype(BF)
        grow1_low = (grow * ahead).astype(BF)
        grow_scr[p, :, LANES:] = grow1_low
        got = jnp.dot(ds, grow1_low, preferred_element_type=F32)
        g1_ref[p] = jnp.where(low_half, got[:batch], got[batch:])
    for p in range(GROUP // 2):
        lags = [lag_ref[2 * p + i : 2 * p + i + 1, :] for i in (0, 1)]
        high = [lag.astype(BF).astype(F32) for lag in lags]
        rest = jnp.where(lagrow == 2, lags[0] - high[0], lags[1] - high[1])
        stack = jnp.where(lagrow == 0, high[0], jnp.where(lagrow == 1, high[1], rest))
        stack = jnp.where(lagrow < 4, stack, 0.0).astype(BF)
        got = jnp.dot(stack, grow_scr[p], preferred_element_type=F32)
        even = got[0:1] + got[2:3]
        uneven = got[1:2] + got[3:4]
        s0_ref[p : p + 1, :] = jnp.where(low_row, even[:, :LANES], uneven[:, :LANES])
        s1_ref[p : p + 1, :] = jnp.where(low_row, even[:, LANES:], uneven[:, LANES:])


def bwd_post_kernel(
    dx_ref, gin_ref, coef_ref, rate_ref, k_ref, v_ref, tail_ref, taps_ref,
    dv_ref, ds_ref, head_ref, gtap_ref, out_ref,
):
    batch = k_ref.shape[0]
    taps = taps_ref.shape[1]
    away = (LANES - 1 - iota2(0)).astype(F32)
    low_half = lax.broadcasted_iota(jnp.int32, (batch, LANES), 1) < LANES // 2
    for p in range(GROUP // 2):
        decay = jnp.exp(-rate_ref[p : p + 1, :] * away).astype(BF)
        g = gin_ref[p] * coef_ref[p : p + 1, :]
        both = jnp.concatenate([jnp.where(low_half, g, 0.0), jnp.where(low_half, 0.0, g)], axis=0)
        cross = lax.dot_general(
            both.astype(BF), decay, (((1,), (1,)), ((), ())), preferred_element_type=F32
        )
        out_ref[pl.ds(2 * p, batch, stride=GROUP), :] = cross[:batch]
        out_ref[pl.ds(2 * p + 1, batch, stride=GROUP), :] = cross[batch:]
    lane = lax.broadcasted_iota(jnp.int32, (GROUP, LANES), 1)
    tail = tail_ref[...]
    spread = spread_taps(taps_ref)
    head = jnp.zeros((GROUP, LANES), F32)
    sums = [jnp.zeros((GROUP, LANES), F32) for _ in range(taps)]
    for b in range(batch):
        block = k_ref[b]
        edge = unpack_tail(tail, b, taps)
        lagged = [block] + [lag_rows(block, edge, i, lane) for i in range(1, taps)]
        shifted = spread[0] * block
        for i in range(1, taps):
            shifted = shifted + spread[i] * lagged[i]
        d_mixed = dx_ref[b] + out_ref[b * GROUP : (b + 1) * GROUP, :]
        dv_ref[b] = (d_mixed * shifted).astype(BF)
        d_shifted = d_mixed * v_ref[b]
        ds_ref[b] = d_shifted
        for i in range(taps):
            sums[i] = sums[i] + d_shifted * lagged[i]
        start = (taps - 1) * b
        head = jnp.where(
            (lane >= start) & (lane < start + taps - 1), pltpu.roll(d_shifted, start, 1), head
        )
    head_ref[...] = head
    packed = jnp.zeros((GROUP, LANES), F32)
    for i in range(taps):
        packed = jnp.where(lane == i, jnp.sum(sums[i], axis=1, keepdims=True), packed)
    gtap_ref[...] = packed


def first_kernel(
    mine_ref, x_ref, gain_ref, wq_ref, wk_ref, wv_ref, normed_ref, q_ref, k_ref, v_ref, tail_ref,
    *, edge
):
    step = pl.program_id(0)
    channels = wq_ref.shape[0]

    @pl.when(step == 0)
    def start():
        tail_ref[...] = jnp.zeros_like(tail_ref)

    seqs = x_ref.shape[0]
    rows = x_ref[...].reshape(seqs * LANES, x_ref.shape[2]).astype(F32)
    center = rows - jnp.mean(rows, axis=-1, keepdims=True)
    spread = jnp.mean(center * center, axis=-1, keepdims=True)
    normed = (center * lax.rsqrt(spread + 1e-05) * gain_ref[...]).astype(BF)
    normed_ref[...] = normed.reshape(normed_ref.shape)
    lane = lax.broadcasted_iota(jnp.int32, (channels, LANES), 1)
    for w_ref, out_ref in ((wq_ref, q_ref), (wk_ref, k_ref), (wv_ref, v_ref)):
        out = lax.dot_general(
            w_ref[...], normed, (((1,), (1,)), ((), ())), preferred_element_type=F32
        )
        for j in range(seqs):
            block = out[:, j * LANES : (j + 1) * LANES]
            out_ref[j] = block
            if out_ref is k_ref:
                at = edge * (step * seqs + j)
                block = pltpu.roll(block, at + edge, 1)
                tail_ref[...] = jnp.where((lane >= at) & (lane < at + edge), block, tail_ref[...])


def last_kernel(
    dq_ref, dv_ref, ds_ref, spill_ref, taps_ref, normed_ref, wq_ref, wk_ref, wv_ref, *rest
):
    piece_refs = rest[:-2]
    grad_ref, gain_ref = rest[-2:]
    step = pl.program_id(0)
    seqs, channels, _ = dq_ref.shape
    taps = taps_ref.shape[1]
    edge = taps - 1

    @pl.when(step == 0)
    def start():
        grad_ref[...] = jnp.zeros_like(grad_ref)
        gain_ref[...] = jnp.zeros_like(gain_ref)

    lane = lax.broadcasted_iota(jnp.int32, (channels, LANES), 1)
    spread = spread_taps(taps_ref)
    sides = []
    for j in range(seqs):
        block = ds_ref[j]
        at = edge * (step * seqs + j)
        after = pltpu.roll(spill_ref[...], (LANES - at) % LANES, 1)
        d_keys = spread[0] * block
        for i in range(1, taps):
            moved = pltpu.roll(jnp.where(lane >= i, block, after), LANES - i, 1)
            d_keys = d_keys + spread[i] * moved
        sides.append(jnp.concatenate([dq_ref[j], d_keys.astype(BF), dv_ref[j]], axis=0))
    both = jnp.concatenate(sides, axis=1)
    normed = normed_ref[...].reshape(seqs * LANES, normed_ref.shape[2])
    grad_ref[: 2 * channels, :] += jnp.dot(both[channels:], normed, preferred_element_type=F32)
    weights = jnp.concatenate([wq_ref[...], wk_ref[...], wv_ref[...]], axis=0)
    rows = lax.dot_general(both, weights, (((0,), (0,)), ((), ())), preferred_element_type=F32)
    gain_ref[...] += jnp.sum(rows * normed.astype(F32), axis=0, keepdims=True)
    for i, piece_ref in enumerate(piece_refs):

        @pl.when(step == i)
        def store(piece_ref=piece_ref):
            piece_ref[...] = rows.reshape(piece_ref.shape)


def first_call(mine, inputs, gain, weights, edge, chunks, parts):
    num_seqs, _, width = inputs.shape
    channels = weights[0].shape[0]
    seqs = num_seqs // (chunks * parts)
    whole = pl.BlockSpec((channels, width), lambda s, m: (0, 0))
    act = pl.BlockSpec((seqs, channels, LANES), lambda s, m: (s, 0, 0))
    rows = pl.BlockSpec((seqs, LANES, width), lambda s, m: (s, 0, 0))
    a = shape(num_seqs, channels, LANES)
    return pl.pallas_call(
        functools.partial(first_kernel, edge=edge),
        grid_spec=pltpu.PrefetchScalarGridSpec(
            num_scalar_prefetch=1,
            grid=(chunks * parts,),
            in_specs=[
                pl.BlockSpec(
                    (seqs, LANES, width),
                    lambda s, m: ((m[0] ^ (s % parts)) * chunks + s // parts, 0, 0),
                ),
                pl.BlockSpec((1, width), lambda s, m: (0, 0)),
                whole,
                whole,
                whole,
            ],
            out_specs=[
                rows,
                act,
                act,
                act,
                pl.BlockSpec((channels, LANES), lambda s, m: (0, 0)),
            ],
        ),
        out_shape=[
            shape(num_seqs, LANES, width, dtype=BF),
            a,
            a,
            a,
            shape(channels, LANES),
        ],
    )(mine[None], inputs, gain[None, :], *weights)


def last_call(dq, dv, ds, spill, tap_rows, normed, weights, pieces, more):
    num_seqs, channels, _ = dq.shape
    taps = tap_rows.shape[1]
    width = normed.shape[2]
    seqs = num_seqs // pieces
    act = pl.BlockSpec((seqs, channels, LANES), lambda s: (s, 0, 0))
    out = pl.pallas_call(
        last_kernel,
        grid=(pieces,),
        in_specs=[
            act,
            act,
            act,
            pl.BlockSpec((channels, LANES), lambda s: (0, 0)),
            pl.BlockSpec((channels, taps), lambda s: (0, 0)),
            pl.BlockSpec((seqs, LANES, width), lambda s: (s, 0, 0)),
        ]
        + [pl.BlockSpec((channels, width), lambda s: (0, 0))] * 3,
        out_specs=[pl.BlockSpec((seqs, LANES, width), lambda s: (0, 0, 0))] * pieces
        + [
            pl.BlockSpec((2 * channels + more, width), lambda s: (0, 0)),
            pl.BlockSpec((1, width), lambda s: (0, 0)),
        ],
        out_shape=[shape(seqs, LANES, width)] * pieces
        + [shape(2 * channels + more, width), shape(1, width)],
    )(dq, dv, ds, spill, tap_rows, normed, *weights)
    return out[:-2], out[-2], out[-1]


def place_kernel(blocks_ref, *refs):
    step = pl.program_id(0)
    for i, piece_ref in enumerate(refs[:-1]):

        @pl.when(step == i)
        def store(piece_ref=piece_ref):
            refs[-1][...] = piece_ref[...]


def place_call(blocks, pieces):
    count = len(pieces)
    piece = pieces[0].shape
    return pl.pallas_call(
        place_kernel,
        grid_spec=pltpu.PrefetchScalarGridSpec(
            num_scalar_prefetch=1,
            grid=(count,),
            in_specs=[pl.BlockSpec(piece, lambda s, b: (0, 0, 0))] * count,
            out_specs=pl.BlockSpec(piece, lambda s, b: (b[s], 0, 0)),
        ),
        out_shape=shape(count * piece[0], *piece[1:]),
    )(blocks, *pieces)


def specs(batch, taps):
    return dict(
        act=pl.BlockSpec((batch, GROUP, LANES), lambda i: (0, i, 0)),
        row=pl.BlockSpec((GROUP, LANES), lambda i: (i, 0)),
        pair=pl.BlockSpec((GROUP // 2, LANES), lambda i: (i, 0)),
        state=pl.BlockSpec((GROUP // 2, batch, LANES), lambda i: (i, 0, 0)),
        taps=pl.BlockSpec((GROUP, taps), lambda i: (i, 0)),
        one=pl.BlockSpec((GROUP, 1), lambda i: (i, 0)),
    )


def shape(*dims, dtype=F32):
    return jax.ShapeDtypeStruct(dims, dtype)


def call(kernel, ins, outs, out_shapes, scratch, channels, args):
    return pl.pallas_call(
        kernel,
        grid=(channels // GROUP,),
        in_specs=ins,
        out_specs=outs,
        out_shape=out_shapes,
        scratch_shapes=scratch,
    )(*args)


def conv_calls(batch, channels, taps):
    s = specs(batch, taps)
    act, row, pair, state, tap, one = (s[n] for n in ("act", "row", "pair", "state", "taps", "one"))
    a = shape(batch, channels, LANES)
    alow = shape(batch, channels, LANES, dtype=BF)
    st = shape(channels // 2, batch, LANES)
    rows = shape(channels, LANES)
    pairs = shape(channels // 2, LANES)
    scr = pltpu.VMEM((batch * GROUP, LANES), F32)

    def fwd_local(k, v, tail, tap_rows, rate, kern):
        return call(fwd_local_kernel, [act, act, row, tap, pair, row], [act, act, state],
                    [a, a, st], [scr, scr], channels, (k, v, tail, tap_rows, rate, kern))

    def fwd_post(y, hin, coef, rate, mixed, q, skip):
        return call(fwd_post_kernel, [act, state, pair, pair, act, act, one],
                    [act, act], [a, alow], [scr], channels, (y, hin, coef, rate, mixed, q, skip))

    def bwd_local(dg, q, so, skip, rate, kern):
        return call(bwd_local_kernel, [act, act, act, one, pair, row],
                    [act, act, act, state], [alow, a, a, st], [scr, scr], channels,
                    (dg, q, so, skip, rate, kern))

    def bwd_lags(d, mixed, rate, part, parts):
        steps = channels // GROUP // parts
        ins = [
            pl.BlockSpec((batch, GROUP, LANES), lambda i: (0, i + part * steps, 0)),
            pl.BlockSpec((batch, GROUP, LANES), lambda i: (0, i + part * steps, 0)),
            pl.BlockSpec((GROUP // 2, LANES), lambda i: (i + part * steps, 0)),
        ]
        count = channels // parts
        sp = shape(count // 2, batch, LANES)
        two = shape(count // 2, LANES)
        return call(bwd_lags_kernel, ins, [state, state, row, pair, pair],
                    [sp, sp, shape(count, LANES), two, two],
                    [scr, scr, pltpu.VMEM((GROUP // 2, LANES, 2 * batch), BF),
                     pltpu.VMEM((GROUP // 2, LANES, 2 * LANES), BF)], count, (d, mixed, rate))

    def bwd_post(dx, gin, coef, rate, k, v, tail, tap_rows):
        return call(bwd_post_kernel, [act, state, pair, pair, act, act, row, tap],
                    [act, act, row, row], [alow, a, rows, rows], [scr], channels,
                    (dx, gin, coef, rate, k, v, tail, tap_rows))

    return fwd_local, fwd_post, bwd_local, bwd_lags, bwd_post


def passed_along(x, axis, by):
    count = lax.axis_size(axis)
    pairs = [(i, i + by) for i in range(count) if 0 <= i + by < count]
    return lax.ppermute(x, axis, pairs)


def swapped(x, axis, bit):
    return lax.ppermute(x, axis, [(i, i ^ bit) for i in range(lax.axis_size(axis))])


def summed(x, axes):
    for axis in axes:
        bit = 1
        while bit < lax.axis_size(axis):
            x = x + swapped(x, axis, bit)
            bit *= 2
    return x


def carried(own, decay, sign, fill=lambda got, step: got):
    count = lax.axis_size("seq")
    odd = lax.axis_index("seq") % 2 == 1
    rows = own.shape[0] // 2
    fall = jnp.where(odd, decay(1)[rows:], decay(1)[:rows])
    keep = jnp.where(odd, own[rows:], own[:rows])
    got = fill(swapped(jnp.where(odd, own[:rows], own[rows:]), "seq", 1), 0)
    leads = odd if sign < 0 else jnp.logical_not(odd)
    lead = jnp.where(leads, keep, got)
    both = fall * lead + jnp.where(leads, got, keep)
    into = fill(passed_along(both, "seq", 2 * sign), 1)
    reach = 1
    while reach < count // 2 - 1:
        far = jnp.where(odd, decay(2 * reach)[rows:], decay(2 * reach)[:rows])
        whole = both + fall * fall * into
        got = passed_along(whole, "seq", 2 * sign * (reach + 1))
        into = into + far * (fill(got, 2) if reach == 1 else got)
        reach = 2 * reach + 1
    then = fall * into + lead
    stay = jnp.where(leads, into, then)
    back = fill(swapped(jnp.where(leads, then, into), "seq", 1), 3)
    return jnp.concatenate([jnp.where(odd, back, stay), jnp.where(odd, stay, back)], axis=0)


class Link:
    def __init__(self):
        self.waits = ()

    def swap(self, x, *more):
        x, *_ = lax.optimization_barrier((x, *self.waits, *more))
        got = swapped(x, "tp", 2)
        self.waits = (got,)
        return got


def far_total(part):
    own, side = part if isinstance(part, (tuple, list)) else jnp.split(part, 2, axis=0)
    return own + swapped(side, "tp", 1)


def total_steps(x, digits):
    index = lax.axis_index("seq")
    for stride, radix in digits:
        digit = (index // stride) % radix
        rows = x.shape[0] // radix
        got = yield [
            (lax.dynamic_slice_in_dim(x, (digit ^ k) * rows, rows, 0), k * stride)
            for k in range(1, radix)
        ]
        x = sum(got, lax.dynamic_slice_in_dim(x, digit * rows, rows, 0))
    for stride, radix in reversed(digits):
        digit = (index // stride) % radix
        rows = x.shape[0]
        got = yield [(x, k * stride) for k in range(1, radix)]
        whole = jnp.zeros((radix * rows,) + x.shape[1:], x.dtype)
        for k, part in enumerate([x, *got]):
            whole = lax.dynamic_update_slice_in_dim(whole, part, (digit ^ k) * rows, 0)
        x = whole
    return x


class Total:
    def __init__(self, x):
        count = lax.axis_size("seq")
        digits = [(1, 2)]
        while digits[-1][0] * digits[-1][1] < count:
            stride = digits[-1][0] * digits[-1][1]
            digits.append((stride, min(4, count // stride)))
        self.rounds = 2 * len(digits)
        self.steps = total_steps(x, digits)
        self.sends = next(self.steps)

    def run(self, rounds):
        got = ()
        for _ in range(rounds * self.rounds // 4):
            got = tuple(swapped(x, "seq", by) for x, by in self.sends)
            try:
                self.sends = self.steps.send(got)
            except StopIteration as end:
                self.done = end.value
        return got


def centered(rows):
    center = rows - jnp.mean(rows, axis=-1, keepdims=True)
    spread = jnp.mean(center * center, axis=-1, keepdims=True)
    inverse = lax.rsqrt(spread + 1e-05)
    return center * inverse, inverse


def norm_back(unit, inverse, grad, gain):
    scaled = grad * gain
    mean_one = jnp.mean(scaled, axis=-1, keepdims=True)
    mean_two = jnp.mean(scaled * unit, axis=-1, keepdims=True)
    return inverse * (scaled - mean_one - unit * mean_two)


def product(form, left, right):
    return jnp.einsum(form, left, right, preferred_element_type=F32)


def local(
    inputs,
    lengths,
    first_gain,
    query_weight,
    key_weight,
    value_weight,
    shift_taps,
    state_coef,
    state_rate,
    skip_gain,
    project_weight,
    second_gain,
    up_weight,
    down_weight,
    cotangent,
):
    place = lax.axis_index("seq")
    mine = lax.axis_index("tp")
    parts = lax.axis_size("tp")
    assert parts == 4
    num_seqs, block_len, width_all = inputs.shape
    taps = shift_taps.shape[0]
    channels, states = state_coef.shape
    assert block_len == LANES and 2 * states == LANES and channels % GROUP == 0
    edge = taps - 1
    chunks = 2
    size = num_seqs // chunks
    piece = size // parts
    half = 2 * piece
    group_seqs = num_seqs // parts

    def starts():
        for u in range(chunks):
            for r in range(parts):
                yield (mine ^ r) * group_seqs + u * piece

    def groups(x):
        return jnp.concatenate(
            [lax.dynamic_slice_in_dim(x, at, piece, 0) for at in starts()], axis=0
        )

    def placed(pieces):
        blocks = [(mine ^ r) * chunks + u for u in range(chunks) for r in range(parts)]
        return place_call(jnp.stack(blocks), pieces)

    own_inputs = [
        lax.dynamic_slice_in_dim(inputs, mine * group_seqs + u * piece, piece, 0).astype(F32)
        for u in range(chunks)
    ]

    def nears(x, u):
        return x[u * size : u * size + half]

    def fars(x, u):
        return x[u * size + half : (u + 1) * size]

    def owns(x, u):
        return x[u * size : u * size + piece]

    link = Link()
    lengths = groups(lengths)
    positions = place * block_len + jnp.arange(block_len)
    valid = (positions[None, :] < lengths[:, None])[:, :, None]
    d_mlp = jnp.where(valid, groups(cotangent), 0)
    fwd_local, fwd_post, bwd_local, bwd_lags, bwd_post = conv_calls(num_seqs, channels, taps)
    rate = state_rate.reshape(channels // 2, LANES)
    coef = state_coef.reshape(channels // 2, LANES)
    tap_rows = shift_taps.T
    skip = skip_gain[:, None]
    lag = jnp.arange(LANES).astype(F32)
    kern = jnp.sum(
        state_coef[:, :, None] * jnp.exp(-state_rate[:, :, None] * lag[None, None, :]), axis=1
    )

    def block_decay(count):
        return jnp.exp(-rate * (LANES * count))[:, None, :]

    turned = (query_weight.T, key_weight.T, value_weight.T)
    normed, queries, keys, values, tail = first_call(
        mine, inputs, first_gain, turned, edge, chunks, parts
    )
    tail = passed_along(tail, "seq", 1)
    conv, mixed, own = fwd_local(keys, values, tail, tap_rows, rate, kern)
    def mask_fill(got, step):
        nonlocal d_mlp
        if step == 1:
            got, d_mlp = lax.optimization_barrier((got, d_mlp))
        return got

    before = carried(own, block_decay, 1, mask_fill)
    state_out, gated_out = fwd_post(conv, before, coef, rate, mixed, queries, skip)

    sums = []
    for u in range(chunks):
        far = link.swap(far_total(product("bct,cd->btd", fars(gated_out, u), project_weight)))
        near = far_total(product("bct,cd->btd", nears(gated_out, u), project_weight))
        sums.append((near, far))
    def feed(first, d_out):
        up_act = product("btd,df->btf", first, up_weight)
        hidden, pull = jax.vjp(jax.nn.gelu, up_act)
        hidden = hidden.astype(BF)
        d_hidden = product("btd,fd->btf", d_out, down_weight)
        d_up = pull(d_hidden)[0].astype(BF)
        return hidden, d_up, product("btf,df->btd", d_up, up_weight)

    def scaled(*two):
        return (jnp.concatenate(two, axis=0) * second_gain).astype(BF)

    residuals = []
    units = []
    seconds = []
    fed = []
    for u in range(chunks):
        near, far = sums[u]
        residual = own_inputs[u] + (near + far)
        unit = centered(residual)
        residuals.append(residual)
        units.append(unit)
        side = swapped(unit[0], "tp", 1)
        far = link.swap(unit[0])
        near_fed = feed(scaled(unit[0], side), nears(d_mlp, u))
        if u + 1 < chunks:
            link.waits += tuple(near_fed)
        else:
            far, near_fed, fed = lax.optimization_barrier((far, near_fed, fed))
        second_far = scaled(far, swapped(far, "tp", 1))
        far_fed = feed(second_far, fars(d_mlp, u))
        seconds += [scaled(unit[0], side), second_far]
        fed += [near_fed, far_fed]
    sums = []
    for u in range(chunks):
        far = link.swap(far_total(fed[2 * u + 1][2]))
        sums.append((far_total(fed[2 * u][2]), far))
    hiddens = [x[0] for x in fed]
    d_ups = [x[1] for x in fed]
    hidden = jnp.concatenate(hiddens, axis=0)
    d_up = jnp.concatenate(d_ups, axis=0)
    second = jnp.concatenate(seconds, axis=0)
    grad_down = product("btf,btd->fd", hidden, d_mlp)
    grad_up = product("btd,btf->df", second, d_up)
    link.waits += (grad_up, grad_down)
    early = lax.psum_scatter(
        jnp.concatenate([grad_up, grad_down], axis=0), "seq", scatter_dimension=0, tiled=True
    )
    grad_second = 0.0
    d_norms = []
    groups_back = []
    for u in range(chunks):
        d_second = sums[u][0] + sums[u][1]
        unit, inverse = units[u]
        d_norm = norm_back(unit, inverse, d_second, second_gain)
        grad_second = grad_second + jnp.sum(d_second * unit, axis=(0, 1))
        side = swapped(d_norm, "tp", 1)
        far = link.swap(d_norm)
        groups_back += [d_norm, side, far, swapped(far, "tp", 1)]
        d_norms.append(d_norm)
    lowered = [
        (
            product("btf,fd->btd", hiddens[2 * u], down_weight),
            product("btf,fd->btd", hiddens[2 * u + 1], down_weight),
        )
        for u in range(chunks)
    ]
    groups_back, lowered = lax.optimization_barrier((groups_back, lowered))
    d_resid_low = (jnp.concatenate(groups_back, axis=0) + d_mlp.astype(F32)).astype(BF)
    d_gated = product("btd,cd->bct", d_resid_low, project_weight)
    d_queries, d_state, d_part, back = bwd_local(
        d_gated, queries, state_out, skip, rate, kern[:, ::-1]
    )
    outs = []
    out_groups = []

    def lower(u):
        far = link.swap(far_total(lowered[u][1]))
        outs.append(far_total(lowered[u][0]) + far)
        return far

    def give_out(u):
        out = jnp.where(owns(valid, u), residuals[u] + outs[u], 0.0)
        side = swapped(out, "tp", 1)
        far = link.swap(out)
        out_groups.extend([out, side, far, swapped(far, "tp", 1)])
        return far

    grad_project = product("bct,btd->cd", gated_out, d_resid_low)
    grad_query = product("bct,btd->cd", d_queries, normed)
    lagged = bwd_lags(d_state, mixed, rate, 0, 1)

    def back_fill(got, step):
        nonlocal lagged, grad_project, grad_query, early
        if step == 0:
            got, _ = lax.optimization_barrier((got, lower(0)))
        elif step == 1:
            got, grad_project, grad_query, early = lax.optimization_barrier(
                (got, grad_project, grad_query, early)
            )
        elif step == 2:
            got, lagged, _ = lax.optimization_barrier((got, lagged, lower(1)))
        else:
            got, _ = lax.optimization_barrier((got, give_out(0)))
        return got

    after = carried(back, block_decay, -1, back_fill)
    early = lax.all_gather(early, "seq", axis=0, tiled=True)
    give_out(1)
    block_out = placed(out_groups)
    others = Total(jnp.concatenate([grad_project, grad_query], axis=0))
    first_got = others.run(1)
    d_values, d_shifted, head, grad_taps = bwd_post(
        d_part, after, coef, rate, keys, values, tail, tap_rows
    )
    spill = passed_along(head, "seq", -1)
    spill, block_out, _ = lax.optimization_barrier((spill, block_out, first_got))
    link.waits += others.run(1)
    pieces, main, grad_first = last_call(
        d_queries, d_values, d_shifted, spill, tap_rows, normed, turned, chunks * parts, 64
    )
    own_lag, back_lag, lags, near, near_lag = lagged
    grow = jnp.exp(rate)
    grad_coef = jnp.sum(before * back, axis=1) + grow * near
    grad_rate = -coef * (
        jnp.sum(
            back_lag * before + after * (own_lag + LANES * block_decay(1) * before), axis=1
        )
        + grow * (near_lag - near)
    )
    pairs = channels // 2
    edges = jnp.concatenate([grad_taps[:, :taps].T.reshape(-1), lags[:, 0]])
    edges = jnp.pad(edges, (0, -edges.shape[0] % width_all)).reshape(-1, width_all)
    gains = summed(jnp.concatenate([grad_first / first_gain, grad_second[None, :]]), ("tp",))
    tables = [grad_coef.reshape(-1, width_all), grad_rate.reshape(-1, width_all), gains, edges]
    rows = sum(x.shape[0] for x in tables)
    tables.append(jnp.zeros((64 - rows, width_all), F32))
    main = lax.dynamic_update_slice(main, jnp.concatenate(tables, axis=0), (2 * channels, 0))
    mains = Total(main)
    rows = grad_up.shape[0]
    grad_up, grad_down = early[:rows], early[rows:]
    link.waits += (gains,)
    sums = []
    for u in range(chunks):
        at = parts * u
        far = link.swap(far_total((pieces[at + 2], pieces[at + 3])))
        link.waits += mains.run(1) + others.run(1)
        sums.append((far_total((pieces[at], pieces[at + 1])), far))
    out_groups = []
    for u in range(chunks):
        d_first = sums[u][0] + sums[u][1]
        unit, inverse = centered(own_inputs[u])
        d_rows = d_norms[u] + owns(d_mlp, u).astype(F32)
        d_rows = d_rows + norm_back(unit, inverse, d_first, first_gain)
        side = swapped(d_rows, "tp", 1)
        far = link.swap(d_rows)
        link.waits += mains.run(1) + (() if u else (grad_up, grad_down))
        out_groups += [d_rows, side, far, swapped(far, "tp", 1)]
    grad_inputs = placed(out_groups)
    main = mains.done
    at = 2 * channels
    grad_key, grad_value = main[:channels].T, main[channels:at].T
    rows = pairs * LANES // width_all
    grad_coef = main[at : at + rows].reshape(channels, states)
    grad_rate = main[at + rows : at + 2 * rows].reshape(channels, states)
    at += 2 * rows
    gains = main[at : at + 2]
    edges = main[at + 2 :].reshape(-1)
    grad_taps = edges[: taps * channels].reshape(taps, channels)
    grad_skip = edges[taps * channels : (taps + 1) * channels]
    grad_project, grad_query = others.done[:channels], others.done[channels:].T
    return (
        block_out,
        grad_inputs,
        gains[0],
        grad_query,
        grad_key,
        grad_value,
        grad_taps,
        grad_coef,
        grad_rate,
        grad_skip,
        grad_project,
        gains[1],
        grad_up,
        grad_down,
    )


def solution(mesh):
    return jax.shard_map(
        local,
        mesh=mesh,
        in_specs=(
            P(None, "seq", None),
            P(),
            P(),
            P(None, "tp"),
            P(None, "tp"),
            P(None, "tp"),
            P(None, "tp"),
            P("tp", None),
            P("tp", None),
            P("tp"),
            P("tp", None),
            P(),
            P(None, "tp"),
            P("tp", None),
            P(None, "seq", None),
        ),
        out_specs=(
            P(None, "seq", None),
            P(None, "seq", None),
            P(),
            P(None, "tp"),
            P(None, "tp"),
            P(None, "tp"),
            P(None, "tp"),
            P("tp", None),
            P("tp", None),
            P("tp"),
            P("tp", None),
            P(),
            P(None, "tp"),
            P("tp", None),
        ),
        check_vma=False,
    )
```

```python
import functools

import jax
import jax.numpy as jnp
from jax import lax
from jax.experimental import pallas as pl
from jax.experimental.pallas import tpu as pltpu
from jax.sharding import PartitionSpec as P

LANES = 128
GROUP = 32
BF = jnp.bfloat16
F32 = jnp.float32


def iota2(axis):
    return lax.broadcasted_iota(jnp.int32, (LANES, LANES), axis)


def strided(ref, c, rows):
    return ref[pl.ds(c, rows, stride=GROUP), :]


def lag_rows(block, edge, offset, lane):
    return pltpu.roll(jnp.where(lane < LANES - offset, block, edge), offset, 1)


def unpack_tail(tail, b, taps):
    return pltpu.roll(tail, (LANES - (taps - 1) * (b + 1)) % LANES, 1)


def spread_taps(taps_ref):
    rows, taps = taps_ref.shape
    return [jnp.broadcast_to(taps_ref[:, i : i + 1], (rows, LANES)) for i in range(taps)]


def shift_sum(block, tail, b, spread, lane):
    edge = unpack_tail(tail, b, len(spread))
    total = spread[0] * block
    for offset in range(1, len(spread)):
        total = total + spread[offset] * lag_rows(block, edge, offset, lane)
    return total


def fwd_local_kernel(
    k_ref, v_ref, tail_ref, taps_ref, rate_ref, kern_ref, y_ref, mixed_ref, h_ref, mix_ref, out_ref
):
    batch = k_ref.shape[0]
    lane = lax.broadcasted_iota(jnp.int32, (GROUP, LANES), 1)
    tail = tail_ref[...]
    spread = spread_taps(taps_ref)
    for b in range(batch):
        mixed = shift_sum(k_ref[b], tail, b, spread, lane) * v_ref[b]
        mix_ref[b * GROUP : (b + 1) * GROUP, :] = mixed
        mixed_ref[b] = mixed
    row = iota2(0)
    col = iota2(1)
    away = (LANES - 1 - row).astype(F32)
    low_half = lax.broadcasted_iota(jnp.int32, (batch, LANES), 1) < LANES // 2
    for p in range(GROUP // 2):
        xs = []
        for c in (2 * p, 2 * p + 1):
            x = strided(mix_ref, c, batch).astype(BF)
            xs.append(x)
            toep = jnp.broadcast_to(kern_ref[c : c + 1, :], (LANES, LANES))
            toep = pltpu.roll(toep, 0, 1, stride=1, stride_axis=0)
            toep = jnp.where(col >= row, toep, 0.0).astype(BF)
            out_ref[pl.ds(c, batch, stride=GROUP), :] = jnp.dot(
                x, toep, preferred_element_type=F32
            )
        decay = jnp.exp(-rate_ref[p : p + 1, :] * away)
        both = jnp.concatenate(xs, axis=0)
        grown = jnp.dot(both, decay.astype(BF), preferred_element_type=F32)
        h_ref[p] = jnp.where(low_half, grown[:batch], grown[batch:])
    for b in range(batch):
        y_ref[b] = out_ref[b * GROUP : (b + 1) * GROUP, :]


def fwd_post_kernel(
    y_ref, hin_ref, coef_ref, rate_ref, mixed_ref, q_ref, skip_ref, state_ref, gated_ref, out_ref
):
    batch = y_ref.shape[0]
    ahead = (iota2(0) + 1).astype(F32)
    low_half = lax.broadcasted_iota(jnp.int32, (batch, LANES), 1) < LANES // 2
    for p in range(GROUP // 2):
        grow = jnp.exp(-rate_ref[p : p + 1, :] * ahead).astype(BF)
        h = hin_ref[p] * coef_ref[p : p + 1, :]
        both = jnp.concatenate([jnp.where(low_half, h, 0.0), jnp.where(low_half, 0.0, h)], axis=0)
        cross = lax.dot_general(
            both.astype(BF), grow, (((1,), (1,)), ((), ())), preferred_element_type=F32
        )
        out_ref[pl.ds(2 * p, batch, stride=GROUP), :] = cross[:batch]
        out_ref[pl.ds(2 * p + 1, batch, stride=GROUP), :] = cross[batch:]
    skip = jnp.broadcast_to(skip_ref[...], (GROUP, LANES))
    for b in range(batch):
        state = y_ref[b] + out_ref[b * GROUP : (b + 1) * GROUP, :] + skip * mixed_ref[b]
        state_ref[b] = state
        gated_ref[b] = (q_ref[b] * state).astype(BF)


def bwd_local_kernel(
    dg_ref, q_ref, state_ref, skip_ref, rate_ref, kern_ref, dq_ref, d_ref, dx_ref, g_ref,
    d_scr, out_ref,
):
    batch = dg_ref.shape[0]
    for b in range(batch):
        dg = dg_ref[b]
        dq_ref[b] = (dg * state_ref[b]).astype(BF)
        d = dg * q_ref[b]
        d_ref[b] = d
        d_scr[b * GROUP : (b + 1) * GROUP, :] = d
    row = iota2(0)
    col = iota2(1)
    ahead = (row + 1).astype(F32)
    low_half = lax.broadcasted_iota(jnp.int32, (batch, LANES), 1) < LANES // 2
    for p in range(GROUP // 2):
        ds = []
        for c in (2 * p, 2 * p + 1):
            d = strided(d_scr, c, batch).astype(BF)
            ds.append(d)
            toep = jnp.broadcast_to(kern_ref[c : c + 1, :], (LANES, LANES))
            toep = pltpu.roll(toep, 1, 1, stride=1, stride_axis=0)
            toep = jnp.where(col <= row, toep, 0.0).astype(BF)
            out_ref[pl.ds(c, batch, stride=GROUP), :] = jnp.dot(
                d, toep, preferred_element_type=F32
            )
        grow = jnp.exp(-rate_ref[p : p + 1, :] * ahead)
        got = jnp.dot(jnp.concatenate(ds, axis=0), grow.astype(BF), preferred_element_type=F32)
        g_ref[p] = jnp.where(low_half, got[:batch], got[batch:])
    skip = jnp.broadcast_to(skip_ref[...], (GROUP, LANES))
    for b in range(batch):
        dx_ref[b] = out_ref[b * GROUP : (b + 1) * GROUP, :] + skip * d_ref[b]


def bwd_lags_kernel(
    d_ref, mixed_ref, rate_ref, h1_ref, g1_ref, lag_ref, s0_ref, s1_ref, x_scr, d_scr, turn_scr,
    grow_scr,
):
    batch = d_ref.shape[0]
    for b in range(batch):
        x_scr[b * GROUP : (b + 1) * GROUP, :] = mixed_ref[b]
        d_scr[b * GROUP : (b + 1) * GROUP, :] = d_ref[b]
    row = iota2(0)
    col = iota2(1)
    mirror = jnp.where(row + col == LANES - 1, 1.0, 0.0).astype(BF)
    ahead = (row + 1).astype(F32)
    away = (LANES - 1 - row).astype(F32)
    low_half = lax.broadcasted_iota(jnp.int32, (batch, LANES), 1) < LANES // 2
    low_row = lax.broadcasted_iota(jnp.int32, (1, LANES), 1) < LANES // 2
    lagrow = lax.broadcasted_iota(jnp.int32, (8, LANES), 0)
    for p in range(GROUP // 2):
        xs = jnp.concatenate([strided(x_scr, 2 * p + i, batch) for i in (0, 1)], axis=0).astype(BF)
        turn_scr[p] = jnp.dot(xs, mirror, preferred_element_type=F32).T.astype(BF)
        fall = jnp.exp(-rate_ref[p : p + 1, :] * away) * away
        got = jnp.dot(xs, fall.astype(BF), preferred_element_type=F32)
        h1_ref[p] = jnp.where(low_half, got[:batch], got[batch:])
    for p in range(GROUP // 2):
        ds = jnp.concatenate([strided(d_scr, 2 * p + i, batch) for i in (0, 1)], axis=0).astype(BF)
        for i in (0, 1):
            part = slice(i * batch, (i + 1) * batch)
            pairs = jnp.dot(turn_scr[p, :, part], ds[part], preferred_element_type=F32)
            pairs = jnp.where(col + row >= LANES - 1, pairs, 0.0)
            pairs = pltpu.roll(pairs, 1, 1, stride=1, stride_axis=0)
            lag_ref[2 * p + i : 2 * p + i + 1, :] = jnp.sum(pairs, axis=0, keepdims=True)
        grow = jnp.exp(-rate_ref[p : p + 1, :] * ahead)
        grow_scr[p, :, :LANES] = grow.astype(BF)
        grow1_low = (grow * ahead).astype(BF)
        grow_scr[p, :, LANES:] = grow1_low
        got = jnp.dot(ds, grow1_low, preferred_element_type=F32)
        g1_ref[p] = jnp.where(low_half, got[:batch], got[batch:])
    for p in range(GROUP // 2):
        lags = [lag_ref[2 * p + i : 2 * p + i + 1, :] for i in (0, 1)]
        high = [lag.astype(BF).astype(F32) for lag in lags]
        rest = jnp.where(lagrow == 2, lags[0] - high[0], lags[1] - high[1])
        stack = jnp.where(lagrow == 0, high[0], jnp.where(lagrow == 1, high[1], rest))
        stack = jnp.where(lagrow < 4, stack, 0.0).astype(BF)
        got = jnp.dot(stack, grow_scr[p], preferred_element_type=F32)
        even = got[0:1] + got[2:3]
        uneven = got[1:2] + got[3:4]
        s0_ref[p : p + 1, :] = jnp.where(low_row, even[:, :LANES], uneven[:, :LANES])
        s1_ref[p : p + 1, :] = jnp.where(low_row, even[:, LANES:], uneven[:, LANES:])


def bwd_post_kernel(
    dx_ref, gin_ref, coef_ref, rate_ref, k_ref, v_ref, tail_ref, taps_ref,
    dv_ref, ds_ref, head_ref, gtap_ref, out_ref,
):
    batch = k_ref.shape[0]
    taps = taps_ref.shape[1]
    away = (LANES - 1 - iota2(0)).astype(F32)
    low_half = lax.broadcasted_iota(jnp.int32, (batch, LANES), 1) < LANES // 2
    for p in range(GROUP // 2):
        decay = jnp.exp(-rate_ref[p : p + 1, :] * away).astype(BF)
        g = gin_ref[p] * coef_ref[p : p + 1, :]
        both = jnp.concatenate([jnp.where(low_half, g, 0.0), jnp.where(low_half, 0.0, g)], axis=0)
        cross = lax.dot_general(
            both.astype(BF), decay, (((1,), (1,)), ((), ())), preferred_element_type=F32
        )
        out_ref[pl.ds(2 * p, batch, stride=GROUP), :] = cross[:batch]
        out_ref[pl.ds(2 * p + 1, batch, stride=GROUP), :] = cross[batch:]
    lane = lax.broadcasted_iota(jnp.int32, (GROUP, LANES), 1)
    tail = tail_ref[...]
    spread = spread_taps(taps_ref)
    head = jnp.zeros((GROUP, LANES), F32)
    sums = [jnp.zeros((GROUP, LANES), F32) for _ in range(taps)]
    for b in range(batch):
        block = k_ref[b]
        edge = unpack_tail(tail, b, taps)
        lagged = [block] + [lag_rows(block, edge, i, lane) for i in range(1, taps)]
        shifted = spread[0] * block
        for i in range(1, taps):
            shifted = shifted + spread[i] * lagged[i]
        d_mixed = dx_ref[b] + out_ref[b * GROUP : (b + 1) * GROUP, :]
        dv_ref[b] = (d_mixed * shifted).astype(BF)
        d_shifted = d_mixed * v_ref[b]
        ds_ref[b] = d_shifted
        for i in range(taps):
            sums[i] = sums[i] + d_shifted * lagged[i]
        start = (taps - 1) * b
        head = jnp.where(
            (lane >= start) & (lane < start + taps - 1), pltpu.roll(d_shifted, start, 1), head
        )
    head_ref[...] = head
    packed = jnp.zeros((GROUP, LANES), F32)
    for i in range(taps):
        packed = jnp.where(lane == i, jnp.sum(sums[i], axis=1, keepdims=True), packed)
    gtap_ref[...] = packed


def first_kernel(
    at_ref, x_ref, cot_ref, gain_ref, wq_ref, wk_ref, wv_ref, normed_ref, cut_ref, q_ref, k_ref,
    v_ref, tail_ref, *, edge, chunks, parts
):
    step = pl.program_id(0)
    channels = wq_ref.shape[0]

    @pl.when(step == 0)
    def start():
        tail_ref[...] = jnp.zeros_like(tail_ref)

    seqs = x_ref.shape[0]
    rows = x_ref[...].reshape(seqs * LANES, x_ref.shape[2]).astype(F32)
    center = rows - jnp.mean(rows, axis=-1, keepdims=True)
    spread = jnp.mean(center * center, axis=-1, keepdims=True)
    normed = (center * lax.rsqrt(spread + 1e-05) * gain_ref[...]).astype(BF)
    normed_ref[...] = normed.reshape(normed_ref.shape)
    place = at_ref[1] * LANES + lax.broadcasted_iota(jnp.int32, cot_ref.shape[1:], 0)
    first = 2 + seqs * ((at_ref[0] ^ (step % parts)) * chunks + step // parts)
    for j in range(seqs):
        kept = jnp.where(place < at_ref[first + j], cot_ref[j].astype(F32), 0.0)
        cut_ref[j] = kept.astype(BF)
    lane = lax.broadcasted_iota(jnp.int32, (channels, LANES), 1)
    for w_ref, out_ref in ((wq_ref, q_ref), (wk_ref, k_ref), (wv_ref, v_ref)):
        out = lax.dot_general(
            w_ref[...], normed, (((1,), (1,)), ((), ())), preferred_element_type=F32
        )
        for j in range(seqs):
            block = out[:, j * LANES : (j + 1) * LANES]
            out_ref[j] = block
            if out_ref is k_ref:
                at = edge * (step * seqs + j)
                block = pltpu.roll(block, at + edge, 1)
                tail_ref[...] = jnp.where((lane >= at) & (lane < at + edge), block, tail_ref[...])


def last_kernel(
    dq_ref, dv_ref, ds_ref, spill_ref, taps_ref, normed_ref, wq_ref, wk_ref, wv_ref, *rest
):
    piece_refs = rest[:-2]
    grad_ref, gain_ref = rest[-2:]
    step = pl.program_id(0)
    seqs, channels, _ = dq_ref.shape
    taps = taps_ref.shape[1]
    edge = taps - 1

    @pl.when(step == 0)
    def start():
        grad_ref[...] = jnp.zeros_like(grad_ref)
        gain_ref[...] = jnp.zeros_like(gain_ref)

    lane = lax.broadcasted_iota(jnp.int32, (channels, LANES), 1)
    spread = spread_taps(taps_ref)
    sides = []
    for j in range(seqs):
        block = ds_ref[j]
        at = edge * (step * seqs + j)
        after = pltpu.roll(spill_ref[...], (LANES - at) % LANES, 1)
        d_keys = spread[0] * block
        for i in range(1, taps):
            moved = pltpu.roll(jnp.where(lane >= i, block, after), LANES - i, 1)
            d_keys = d_keys + spread[i] * moved
        sides.append(jnp.concatenate([dq_ref[j], d_keys.astype(BF), dv_ref[j]], axis=0))
    both = jnp.concatenate(sides, axis=1)
    normed = normed_ref[...].reshape(seqs * LANES, normed_ref.shape[2])
    grad_ref[: 2 * channels, :] += jnp.dot(both[channels:], normed, preferred_element_type=F32)
    weights = jnp.concatenate([wq_ref[...], wk_ref[...], wv_ref[...]], axis=0)
    rows = lax.dot_general(both, weights, (((0,), (0,)), ((), ())), preferred_element_type=F32)
    gain_ref[...] += jnp.sum(rows * normed.astype(F32), axis=0, keepdims=True)
    for i, piece_ref in enumerate(piece_refs):

        @pl.when(step == i)
        def store(piece_ref=piece_ref):
            piece_ref[...] = rows.reshape(piece_ref.shape)


def first_call(at, inputs, cotangent, gain, weights, edge, chunks, parts):
    num_seqs, _, width = inputs.shape
    channels = weights[0].shape[0]
    seqs = num_seqs // (chunks * parts)
    whole = pl.BlockSpec((channels, width), lambda s, m: (0, 0))
    act = pl.BlockSpec((seqs, channels, LANES), lambda s, m: (s, 0, 0))
    rows = pl.BlockSpec((seqs, LANES, width), lambda s, m: (s, 0, 0))
    a = shape(num_seqs, channels, LANES)
    own = pl.BlockSpec(
        (seqs, LANES, width),
        lambda s, m: ((m[0] ^ (s % parts)) * chunks + s // parts, 0, 0),
    )
    return pl.pallas_call(
        functools.partial(first_kernel, edge=edge, chunks=chunks, parts=parts),
        grid_spec=pltpu.PrefetchScalarGridSpec(
            num_scalar_prefetch=1,
            grid=(chunks * parts,),
            in_specs=[
                own,
                own,
                pl.BlockSpec((1, width), lambda s, m: (0, 0)),
                whole,
                whole,
                whole,
            ],
            out_specs=[
                rows,
                rows,
                act,
                act,
                act,
                pl.BlockSpec((channels, LANES), lambda s, m: (0, 0)),
            ],
        ),
        out_shape=[
            shape(num_seqs, LANES, width, dtype=BF),
            shape(num_seqs, LANES, width, dtype=BF),
            a,
            a,
            a,
            shape(channels, LANES),
        ],
    )(at, inputs, cotangent, gain[None, :], *weights)


def last_call(dq, dv, ds, spill, tap_rows, normed, weights, pieces, more):
    num_seqs, channels, _ = dq.shape
    taps = tap_rows.shape[1]
    width = normed.shape[2]
    seqs = num_seqs // pieces
    act = pl.BlockSpec((seqs, channels, LANES), lambda s: (s, 0, 0))
    out = pl.pallas_call(
        last_kernel,
        grid=(pieces,),
        in_specs=[
            act,
            act,
            act,
            pl.BlockSpec((channels, LANES), lambda s: (0, 0)),
            pl.BlockSpec((channels, taps), lambda s: (0, 0)),
            pl.BlockSpec((seqs, LANES, width), lambda s: (s, 0, 0)),
        ]
        + [pl.BlockSpec((channels, width), lambda s: (0, 0))] * 3,
        out_specs=[pl.BlockSpec((seqs, LANES, width), lambda s: (0, 0, 0))] * pieces
        + [
            pl.BlockSpec((2 * channels + more, width), lambda s: (0, 0)),
            pl.BlockSpec((1, width), lambda s: (0, 0)),
        ],
        out_shape=[shape(seqs, LANES, width)] * pieces
        + [shape(2 * channels + more, width), shape(1, width)],
    )(dq, dv, ds, spill, tap_rows, normed, *weights)
    return out[:-2], out[-2], out[-1]


def place_kernel(blocks_ref, *refs, count):
    step = pl.program_id(0)
    for i, piece_ref in enumerate(refs[:count]):

        @pl.when(step == i)
        def store(piece_ref=piece_ref):
            refs[-1][...] = piece_ref[...]


def place_call(blocks, pieces, rows, whole=None):
    count = len(pieces)
    piece = pieces[0].shape
    old = () if whole is None else (whole,)
    return pl.pallas_call(
        functools.partial(place_kernel, count=count),
        grid_spec=pltpu.PrefetchScalarGridSpec(
            num_scalar_prefetch=1,
            grid=(count,),
            in_specs=[pl.BlockSpec(piece, lambda s, b: (0, 0, 0))] * count
            + [pl.BlockSpec(memory_space=pl.ANY)] * len(old),
            out_specs=pl.BlockSpec(piece, lambda s, b: (b[s], 0, 0)),
        ),
        out_shape=shape(rows, *piece[1:]),
        input_output_aliases={count + 1: 0} if old else {},
    )(blocks, *pieces, *old)


def specs(batch, taps):
    return dict(
        act=pl.BlockSpec((batch, GROUP, LANES), lambda i: (0, i, 0)),
        row=pl.BlockSpec((GROUP, LANES), lambda i: (i, 0)),
        pair=pl.BlockSpec((GROUP // 2, LANES), lambda i: (i, 0)),
        state=pl.BlockSpec((GROUP // 2, batch, LANES), lambda i: (i, 0, 0)),
        taps=pl.BlockSpec((GROUP, taps), lambda i: (i, 0)),
        one=pl.BlockSpec((GROUP, 1), lambda i: (i, 0)),
    )


def shape(*dims, dtype=F32):
    return jax.ShapeDtypeStruct(dims, dtype)


def call(kernel, ins, outs, out_shapes, scratch, channels, args):
    return pl.pallas_call(
        kernel,
        grid=(channels // GROUP,),
        in_specs=ins,
        out_specs=outs,
        out_shape=out_shapes,
        scratch_shapes=scratch,
    )(*args)


def conv_calls(batch, channels, taps):
    s = specs(batch, taps)
    act, row, pair, state, tap, one = (s[n] for n in ("act", "row", "pair", "state", "taps", "one"))
    a = shape(batch, channels, LANES)
    alow = shape(batch, channels, LANES, dtype=BF)
    st = shape(channels // 2, batch, LANES)
    rows = shape(channels, LANES)
    pairs = shape(channels // 2, LANES)
    scr = pltpu.VMEM((batch * GROUP, LANES), F32)

    def fwd_local(k, v, tail, tap_rows, rate, kern):
        return call(fwd_local_kernel, [act, act, row, tap, pair, row], [act, act, state],
                    [a, a, st], [scr, scr], channels, (k, v, tail, tap_rows, rate, kern))

    def fwd_post(y, hin, coef, rate, mixed, q, skip):
        return call(fwd_post_kernel, [act, state, pair, pair, act, act, one],
                    [act, act], [a, alow], [scr], channels, (y, hin, coef, rate, mixed, q, skip))

    def bwd_local(dg, q, so, skip, rate, kern):
        return call(bwd_local_kernel, [act, act, act, one, pair, row],
                    [act, act, act, state], [alow, a, a, st], [scr, scr], channels,
                    (dg, q, so, skip, rate, kern))

    def bwd_lags(d, mixed, rate, part, parts):
        steps = channels // GROUP // parts
        ins = [
            pl.BlockSpec((batch, GROUP, LANES), lambda i: (0, i + part * steps, 0)),
            pl.BlockSpec((batch, GROUP, LANES), lambda i: (0, i + part * steps, 0)),
            pl.BlockSpec((GROUP // 2, LANES), lambda i: (i + part * steps, 0)),
        ]
        count = channels // parts
        sp = shape(count // 2, batch, LANES)
        two = shape(count // 2, LANES)
        return call(bwd_lags_kernel, ins, [state, state, row, pair, pair],
                    [sp, sp, shape(count, LANES), two, two],
                    [scr, scr, pltpu.VMEM((GROUP // 2, LANES, 2 * batch), BF),
                     pltpu.VMEM((GROUP // 2, LANES, 2 * LANES), BF)], count, (d, mixed, rate))

    def bwd_post(dx, gin, coef, rate, k, v, tail, tap_rows):
        return call(bwd_post_kernel, [act, state, pair, pair, act, act, row, tap],
                    [act, act, row, row], [alow, a, rows, rows], [scr], channels,
                    (dx, gin, coef, rate, k, v, tail, tap_rows))

    return fwd_local, fwd_post, bwd_local, bwd_lags, bwd_post


def passed_along(x, axis, by):
    count = lax.axis_size(axis)
    pairs = [(i, i + by) for i in range(count) if 0 <= i + by < count]
    return lax.ppermute(x, axis, pairs)


def swapped(x, axis, bit):
    return lax.ppermute(x, axis, [(i, i ^ bit) for i in range(lax.axis_size(axis))])


def summed(x, axes):
    for axis in axes:
        bit = 1
        while bit < lax.axis_size(axis):
            x = x + swapped(x, axis, bit)
            bit *= 2
    return x


def carried(own, decay, sign, fill=lambda got, step: got):
    count = lax.axis_size("seq")
    odd = lax.axis_index("seq") % 2 == 1
    rows = own.shape[0] // 2
    fall = jnp.where(odd, decay(1)[rows:], decay(1)[:rows])
    keep = jnp.where(odd, own[rows:], own[:rows])
    got = fill(swapped(jnp.where(odd, own[:rows], own[rows:]), "seq", 1), 0)
    leads = odd if sign < 0 else jnp.logical_not(odd)
    lead = jnp.where(leads, keep, got)
    both = fall * lead + jnp.where(leads, got, keep)
    into = fill(passed_along(both, "seq", 2 * sign), 1)
    reach = 1
    while reach < count // 2 - 1:
        far = jnp.where(odd, decay(2 * reach)[rows:], decay(2 * reach)[:rows])
        whole = both + fall * fall * into
        got = passed_along(whole, "seq", 2 * sign * (reach + 1))
        into = into + far * (fill(got, 2) if reach == 1 else got)
        reach = 2 * reach + 1
    then = fall * into + lead
    stay = jnp.where(leads, into, then)
    back = fill(swapped(jnp.where(leads, then, into), "seq", 1), 3)
    return jnp.concatenate([jnp.where(odd, back, stay), jnp.where(odd, stay, back)], axis=0)


class Link:
    def __init__(self):
        self.waits = ()
        self.last = ()

    def swap(self, x, *more, free=False):
        x, *_ = lax.optimization_barrier((x, *self.waits, *(() if free else self.last), *more))
        got = swapped(x, "tp", 2)
        self.waits = ()
        self.last = (got,)
        self.sent = x
        return got


def far_total(part):
    own, side = part if isinstance(part, (tuple, list)) else jnp.split(part, 2, axis=0)
    return own + swapped(side, "tp", 1)


def total_steps(x, digits):
    index = lax.axis_index("seq")
    for stride, radix in digits:
        digit = (index // stride) % radix
        rows = x.shape[0] // radix
        got = yield [
            (lax.dynamic_slice_in_dim(x, (digit ^ k) * rows, rows, 0), k * stride)
            for k in range(1, radix)
        ]
        x = sum(got, lax.dynamic_slice_in_dim(x, digit * rows, rows, 0))
    for stride, radix in reversed(digits):
        digit = (index // stride) % radix
        rows = x.shape[0]
        got = yield [(x, k * stride) for k in range(1, radix)]
        whole = jnp.zeros((radix * rows,) + x.shape[1:], x.dtype)
        for k, part in enumerate([x, *got]):
            whole = lax.dynamic_update_slice_in_dim(whole, part, (digit ^ k) * rows, 0)
        x = whole
    return x


class Total:
    def __init__(self, x):
        count = lax.axis_size("seq")
        digits = [(1, 2)]
        while digits[-1][0] * digits[-1][1] < count:
            stride = digits[-1][0] * digits[-1][1]
            digits.append((stride, min(4, count // stride)))
        self.rounds = 2 * len(digits)
        self.steps = total_steps(x, digits)
        self.sends = next(self.steps)

    def run(self, rounds, after=()):
        got = ()
        self.sends = [(lax.optimization_barrier((x, after))[0], by) for x, by in self.sends]
        for _ in range(rounds * self.rounds // 4):
            got = tuple(swapped(x, "seq", by) for x, by in self.sends)
            try:
                self.sends = self.steps.send(got)
            except StopIteration as end:
                self.done = end.value
        return got


def centered(rows):
    center = rows - jnp.mean(rows, axis=-1, keepdims=True)
    spread = jnp.mean(center * center, axis=-1, keepdims=True)
    inverse = lax.rsqrt(spread + 1e-05)
    return center * inverse, inverse


def norm_back(unit, inverse, grad, gain):
    scaled = grad * gain
    mean_one = jnp.mean(scaled, axis=-1, keepdims=True)
    mean_two = jnp.mean(scaled * unit, axis=-1, keepdims=True)
    return inverse * (scaled - mean_one - unit * mean_two)


def product(form, left, right):
    return jnp.einsum(form, left, right, preferred_element_type=F32)


def local(
    inputs,
    lengths,
    first_gain,
    query_weight,
    key_weight,
    value_weight,
    shift_taps,
    state_coef,
    state_rate,
    skip_gain,
    project_weight,
    second_gain,
    up_weight,
    down_weight,
    cotangent,
):
    place = lax.axis_index("seq")
    mine = lax.axis_index("tp")
    parts = lax.axis_size("tp")
    assert parts == 4
    num_seqs, block_len, width_all = inputs.shape
    taps = shift_taps.shape[0]
    channels, states = state_coef.shape
    assert block_len == LANES and 2 * states == LANES and channels % GROUP == 0
    edge = taps - 1
    chunks = 2
    size = num_seqs // chunks
    piece = size // parts
    half = 2 * piece
    group_seqs = num_seqs // parts

    def starts():
        for u in range(chunks):
            for r in range(parts):
                yield (mine ^ r) * group_seqs + u * piece

    def groups(x):
        return jnp.concatenate(
            [lax.dynamic_slice_in_dim(x, at, piece, 0) for at in starts()], axis=0
        )

    def placed(pieces, u, whole=None):
        blocks = jnp.stack([(mine ^ r) * chunks + u for r in range(parts)])
        return place_call(blocks, pieces, num_seqs, whole)

    own_inputs = [
        lax.dynamic_slice_in_dim(inputs, mine * group_seqs + u * piece, piece, 0).astype(F32)
        for u in range(chunks)
    ]

    def nears(x, u):
        return x[u * size : u * size + half]

    def fars(x, u):
        return x[u * size + half : (u + 1) * size]

    def owns(x, u):
        return x[u * size : u * size + piece]

    link = Link()
    ends = groups(lengths)
    positions = place * block_len + jnp.arange(block_len)
    valid = (positions[None, :] < ends[:, None])[:, :, None]
    fwd_local, fwd_post, bwd_local, bwd_lags, bwd_post = conv_calls(num_seqs, channels, taps)
    rate = state_rate.reshape(channels // 2, LANES)
    coef = state_coef.reshape(channels // 2, LANES)
    tap_rows = shift_taps.T
    skip = skip_gain[:, None]
    lag = jnp.arange(LANES).astype(F32)
    kern = jnp.sum(
        state_coef[:, :, None] * jnp.exp(-state_rate[:, :, None] * lag[None, None, :]), axis=1
    )

    def block_decay(count):
        return jnp.exp(-rate * (LANES * count))[:, None, :]

    turned = (query_weight.T, key_weight.T, value_weight.T)
    at = jnp.concatenate([jnp.stack([mine, place]), lengths])
    normed, d_mlp, queries, keys, values, tail = first_call(
        at, inputs, cotangent, first_gain, turned, edge, chunks, parts
    )
    tail = passed_along(tail, "seq", 1)
    conv, mixed, own = fwd_local(keys, values, tail, tap_rows, rate, kern)
    before = carried(own, block_decay, 1)
    state_out, gated_out = fwd_post(conv, before, coef, rate, mixed, queries, skip)

    sums = []
    for u in range(chunks):
        far = link.swap(far_total(product("bct,cd->btd", fars(gated_out, u), project_weight)))
        near = far_total(product("bct,cd->btd", nears(gated_out, u), project_weight))
        sums.append((near, far))
    def feed(first, d_out):
        up_act = product("btd,df->btf", first, up_weight)
        hidden, pull = jax.vjp(jax.nn.gelu, up_act)
        hidden = hidden.astype(BF)
        d_hidden = product("btd,fd->btf", d_out, down_weight)
        d_up = pull(d_hidden)[0].astype(BF)
        return hidden, d_up, product("btf,df->btd", d_up, up_weight)

    def scaled(*two):
        return (jnp.concatenate(two, axis=0) * second_gain).astype(BF)

    residuals = []
    units = []
    seconds = []
    fed = []
    for u in range(chunks):
        near, far = sums[u]
        residual = own_inputs[u] + (near + far)
        unit = centered(residual)
        residuals.append(residual)
        units.append(unit)
        side = swapped(unit[0], "tp", 1)
        far = link.swap(unit[0], free=u > 0)
        near_fed = feed(scaled(unit[0], side), nears(d_mlp, u))
        far, near_fed, fed = lax.optimization_barrier((far, near_fed, fed))
        second_far = scaled(far, swapped(far, "tp", 1))
        far_fed = feed(second_far, fars(d_mlp, u))
        seconds += [scaled(unit[0], side), second_far]
        fed += [near_fed, far_fed]
    hiddens = [x[0] for x in fed]
    d_ups = [x[1] for x in fed]
    sums = []
    for u in range(chunks):
        far = link.swap(far_total(fed[2 * u + 1][2]), *((early,) if u else ()))
        if u == 0:
            late_mlp, late_up, _ = lax.optimization_barrier((d_mlp, d_ups, link.sent))
            grad_down = product("btf,btd->fd", jnp.concatenate(hiddens, axis=0), late_mlp)
            grad_up = product(
                "btd,btf->df", jnp.concatenate(seconds, axis=0), jnp.concatenate(late_up, axis=0)
            )
            early = jnp.concatenate([grad_up, grad_down], axis=0)
        sums.append((far_total(fed[2 * u][2]), far))
    early = lax.psum_scatter(early, "seq", scatter_dimension=0, tiled=True)
    lowered = [product("btf,fd->btd", hidden, down_weight) for hidden in hiddens]
    grad_second = 0.0
    d_norms = []
    lows = []
    gated = []
    for u in range(chunks):
        d_second = sums[u][0] + sums[u][1]
        unit, inverse = units[u]
        d_norm = norm_back(unit, inverse, d_second, second_gain)
        grad_second = grad_second + jnp.sum(d_second * unit, axis=(0, 1))
        side = swapped(d_norm, "tp", 1)
        far = link.swap(d_norm)
        if u + 1 == chunks:
            far, lowered, lows, gated = lax.optimization_barrier((far, lowered, lows, gated))
        rows = jnp.concatenate([d_norm, side, far, swapped(far, "tp", 1)], axis=0)
        low = (rows + d_mlp[u * size : (u + 1) * size].astype(F32)).astype(BF)
        lows.append(low)
        gated.append(product("btd,cd->bct", low, project_weight))
        d_norms.append(d_norm)
    d_resid_low = jnp.concatenate(lows, axis=0)
    d_gated = jnp.concatenate(gated, axis=0)
    d_queries, d_state, d_part, back = bwd_local(
        d_gated, queries, state_out, skip, rate, kern[:, ::-1]
    )
    outs = []

    def lower(u, after):
        far = link.swap(far_total(lowered[2 * u + 1]), after)
        outs.append(far_total(lowered[2 * u]) + far)
        return far

    block_out = None

    def give_out(u, after):
        nonlocal block_out
        out = jnp.where(owns(valid, u), residuals[u] + outs[u], 0.0)
        side = swapped(out, "tp", 1)
        far = link.swap(out, after)
        block_out = placed([out, side, far, swapped(far, "tp", 1)], u, block_out)
        return far

    grad_project = product("bct,btd->cd", gated_out, d_resid_low)
    grad_query = product("bct,btd->cd", d_queries, normed)
    lagged = bwd_lags(d_state, mixed, rate, 0, 1)
    flying = lower(0, back)

    def back_fill(got, step):
        nonlocal lagged, grad_project, grad_query, early, flying
        if step == 1:
            got, grad_project, _ = lax.optimization_barrier((got, grad_project, flying))
            flying = lower(1, got)
        elif step == 2:
            got, lagged, early, _ = lax.optimization_barrier((got, lagged, early, flying))
            flying = give_out(0, got)
        elif step == 3:
            got, grad_query, _ = lax.optimization_barrier((got, grad_query, flying))
        return got

    after = carried(back, block_decay, -1, back_fill)
    early = lax.all_gather(early, "seq", axis=0, tiled=True)
    flying = give_out(1, after)
    others = Total(jnp.concatenate([grad_project, grad_query], axis=0))
    d_values, d_shifted, head, grad_taps = bwd_post(
        d_part, after, coef, rate, keys, values, tail, tap_rows
    )
    spill = passed_along(head, "seq", -1)
    spill, _ = lax.optimization_barrier((spill, flying))
    others.run(1, spill)
    pieces, main, grad_first = last_call(
        d_queries, d_values, d_shifted, spill, tap_rows, normed, turned, chunks * parts, 64
    )
    own_lag, back_lag, lags, near, near_lag = lagged
    grow = jnp.exp(rate)
    grad_coef = jnp.sum(before * back, axis=1) + grow * near
    grad_rate = -coef * (
        jnp.sum(
            back_lag * before + after * (own_lag + LANES * block_decay(1) * before), axis=1
        )
        + grow * (near_lag - near)
    )
    pairs = channels // 2
    edges = jnp.concatenate([grad_taps[:, :taps].T.reshape(-1), lags[:, 0]])
    edges = jnp.pad(edges, (0, -edges.shape[0] % width_all)).reshape(-1, width_all)
    gains = summed(jnp.concatenate([grad_first / first_gain, grad_second[None, :]]), ("tp",))
    tables = [grad_coef.reshape(-1, width_all), grad_rate.reshape(-1, width_all), gains, edges]
    rows = sum(x.shape[0] for x in tables)
    tables.append(jnp.zeros((64 - rows, width_all), F32))
    main = lax.dynamic_update_slice(main, jnp.concatenate(tables, axis=0), (2 * channels, 0))
    mains = Total(main)
    rows = grad_up.shape[0]
    grad_up, grad_down = early[:rows], early[rows:]
    link.waits += (gains,)
    sums = []
    for u in range(chunks):
        at = parts * u
        far = link.swap(far_total((pieces[at + 2], pieces[at + 3])))
        link.waits += others.run(1, link.sent) + mains.run(1, link.sent) + ((block_out,) if u else ())
        sums.append((far_total((pieces[at], pieces[at + 1])), far))
    grad_inputs = None
    for u in range(chunks):
        d_first = sums[u][0] + sums[u][1]
        unit, inverse = centered(own_inputs[u])
        d_rows = d_norms[u] + owns(d_mlp, u).astype(F32)
        d_rows = d_rows + norm_back(unit, inverse, d_first, first_gain)
        side = swapped(d_rows, "tp", 1)
        far = link.swap(d_rows)
        link.waits += mains.run(1, link.sent)
        if u == 0:
            link.waits += (*others.run(1, link.sent), grad_up, grad_down)
        if u:
            far, grad_inputs = lax.optimization_barrier((far, grad_inputs))
        grad_inputs = placed([d_rows, side, far, swapped(far, "tp", 1)], u, grad_inputs)
    main = mains.done
    at = 2 * channels
    grad_key, grad_value = main[:channels].T, main[channels:at].T
    rows = pairs * LANES // width_all
    grad_coef = main[at : at + rows].reshape(channels, states)
    grad_rate = main[at + rows : at + 2 * rows].reshape(channels, states)
    at += 2 * rows
    gains = main[at : at + 2]
    edges = main[at + 2 :].reshape(-1)
    grad_taps = edges[: taps * channels].reshape(taps, channels)
    grad_skip = edges[taps * channels : (taps + 1) * channels]
    grad_project, grad_query = others.done[:channels], others.done[channels:].T
    return (
        block_out,
        grad_inputs,
        gains[0],
        grad_query,
        grad_key,
        grad_value,
        grad_taps,
        grad_coef,
        grad_rate,
        grad_skip,
        grad_project,
        gains[1],
        grad_up,
        grad_down,
    )


def solution(mesh):
    return jax.shard_map(
        local,
        mesh=mesh,
        in_specs=(
            P(None, "seq", None),
            P(),
            P(),
            P(None, "tp"),
            P(None, "tp"),
            P(None, "tp"),
            P(None, "tp"),
            P("tp", None),
            P("tp", None),
            P("tp"),
            P("tp", None),
            P(),
            P(None, "tp"),
            P("tp", None),
            P(None, "seq", None),
        ),
        out_specs=(
            P(None, "seq", None),
            P(None, "seq", None),
            P(),
            P(None, "tp"),
            P(None, "tp"),
            P(None, "tp"),
            P(None, "tp"),
            P("tp", None),
            P("tp", None),
            P("tp"),
            P("tp", None),
            P(),
            P(None, "tp"),
            P("tp", None),
        ),
        check_vma=False,
    )
```

```python
import functools

import jax
import jax.numpy as jnp
from jax import lax
from jax.experimental import pallas as pl
from jax.experimental.pallas import tpu as pltpu
from jax.sharding import PartitionSpec as P

LANES = 128
GROUP = 64
BF = jnp.bfloat16
F32 = jnp.float32


def iota2(axis):
    return lax.broadcasted_iota(jnp.int32, (LANES, LANES), axis)


def strided(ref, c, rows):
    return ref[pl.ds(c, rows, stride=GROUP), :]


def lag_rows(block, edge, offset, lane):
    return pltpu.roll(jnp.where(lane < LANES - offset, block, edge), offset, 1)


def unpack_tail(tail, b, taps):
    return pltpu.roll(tail, (LANES - (taps - 1) * (b + 1)) % LANES, 1)


def spread_taps(taps_ref):
    rows, taps = taps_ref.shape
    return [jnp.broadcast_to(taps_ref[:, i : i + 1], (rows, LANES)) for i in range(taps)]


def shift_sum(block, tail, b, spread, lane):
    edge = unpack_tail(tail, b, len(spread))
    total = spread[0] * block
    for offset in range(1, len(spread)):
        total = total + spread[offset] * lag_rows(block, edge, offset, lane)
    return total


def fwd_local_kernel(
    k_ref, v_ref, tail_ref, taps_ref, rate_ref, kern_ref, y_ref, mixed_ref, h_ref, mix_ref, out_ref
):
    batch = k_ref.shape[0]
    lane = lax.broadcasted_iota(jnp.int32, (GROUP, LANES), 1)
    tail = tail_ref[...]
    spread = spread_taps(taps_ref)
    for b in range(batch):
        mixed = shift_sum(k_ref[b], tail, b, spread, lane) * v_ref[b]
        mix_ref[b * GROUP : (b + 1) * GROUP, :] = mixed
        mixed_ref[b] = mixed
    row = iota2(0)
    col = iota2(1)
    away = (LANES - 1 - row).astype(F32)
    low_half = lax.broadcasted_iota(jnp.int32, (batch, LANES), 1) < LANES // 2
    for p in range(GROUP // 2):
        xs = []
        for c in (2 * p, 2 * p + 1):
            x = strided(mix_ref, c, batch).astype(BF)
            xs.append(x)
            toep = jnp.broadcast_to(kern_ref[c : c + 1, :], (LANES, LANES))
            toep = pltpu.roll(toep, 0, 1, stride=1, stride_axis=0)
            toep = jnp.where(col >= row, toep, 0.0).astype(BF)
            out_ref[pl.ds(c, batch, stride=GROUP), :] = jnp.dot(
                x, toep, preferred_element_type=F32
            )
        decay = jnp.exp(-rate_ref[p : p + 1, :] * away)
        both = jnp.concatenate(xs, axis=0)
        grown = jnp.dot(both, decay.astype(BF), preferred_element_type=F32)
        h_ref[p] = jnp.where(low_half, grown[:batch], grown[batch:])
    for b in range(batch):
        y_ref[b] = out_ref[b * GROUP : (b + 1) * GROUP, :]


def fwd_post_kernel(
    y_ref, hin_ref, coef_ref, rate_ref, mixed_ref, q_ref, skip_ref, state_ref, gated_ref, out_ref
):
    batch = y_ref.shape[0]
    ahead = (iota2(0) + 1).astype(F32)
    low_half = lax.broadcasted_iota(jnp.int32, (batch, LANES), 1) < LANES // 2
    for p in range(GROUP // 2):
        grow = jnp.exp(-rate_ref[p : p + 1, :] * ahead).astype(BF)
        h = hin_ref[p] * coef_ref[p : p + 1, :]
        both = jnp.concatenate([jnp.where(low_half, h, 0.0), jnp.where(low_half, 0.0, h)], axis=0)
        cross = lax.dot_general(
            both.astype(BF), grow, (((1,), (1,)), ((), ())), preferred_element_type=F32
        )
        out_ref[pl.ds(2 * p, batch, stride=GROUP), :] = cross[:batch]
        out_ref[pl.ds(2 * p + 1, batch, stride=GROUP), :] = cross[batch:]
    skip = jnp.broadcast_to(skip_ref[...], (GROUP, LANES))
    for b in range(batch):
        state = y_ref[b] + out_ref[b * GROUP : (b + 1) * GROUP, :] + skip * mixed_ref[b]
        state_ref[b] = state
        gated_ref[b] = (q_ref[b] * state).astype(BF)


def bwd_local_kernel(
    dg_ref, q_ref, state_ref, skip_ref, rate_ref, kern_ref, dq_ref, d_ref, dx_ref, g_ref,
    d_scr, out_ref,
):
    batch = dg_ref.shape[0]
    for b in range(batch):
        dg = dg_ref[b]
        dq_ref[b] = (dg * state_ref[b]).astype(BF)
        d = dg * q_ref[b]
        d_ref[b] = d
        d_scr[b * GROUP : (b + 1) * GROUP, :] = d
    row = iota2(0)
    col = iota2(1)
    ahead = (row + 1).astype(F32)
    low_half = lax.broadcasted_iota(jnp.int32, (batch, LANES), 1) < LANES // 2
    for p in range(GROUP // 2):
        ds = []
        for c in (2 * p, 2 * p + 1):
            d = strided(d_scr, c, batch).astype(BF)
            ds.append(d)
            toep = jnp.broadcast_to(kern_ref[c : c + 1, :], (LANES, LANES))
            toep = pltpu.roll(toep, 1, 1, stride=1, stride_axis=0)
            toep = jnp.where(col <= row, toep, 0.0).astype(BF)
            out_ref[pl.ds(c, batch, stride=GROUP), :] = jnp.dot(
                d, toep, preferred_element_type=F32
            )
        grow = jnp.exp(-rate_ref[p : p + 1, :] * ahead)
        got = jnp.dot(jnp.concatenate(ds, axis=0), grow.astype(BF), preferred_element_type=F32)
        g_ref[p] = jnp.where(low_half, got[:batch], got[batch:])
    skip = jnp.broadcast_to(skip_ref[...], (GROUP, LANES))
    for b in range(batch):
        dx_ref[b] = out_ref[b * GROUP : (b + 1) * GROUP, :] + skip * d_ref[b]


def bwd_lags_kernel(
    d_ref, mixed_ref, rate_ref, h1_ref, g1_ref, lag_ref, s0_ref, s1_ref, x_scr, d_scr, turn_scr,
    grow_scr,
):
    batch = d_ref.shape[0]
    for b in range(batch):
        x_scr[b * GROUP : (b + 1) * GROUP, :] = mixed_ref[b]
        d_scr[b * GROUP : (b + 1) * GROUP, :] = d_ref[b]
    row = iota2(0)
    col = iota2(1)
    mirror = jnp.where(row + col == LANES - 1, 1.0, 0.0).astype(BF)
    ahead = (row + 1).astype(F32)
    away = (LANES - 1 - row).astype(F32)
    low_half = lax.broadcasted_iota(jnp.int32, (batch, LANES), 1) < LANES // 2
    low_row = lax.broadcasted_iota(jnp.int32, (1, LANES), 1) < LANES // 2
    lagrow = lax.broadcasted_iota(jnp.int32, (8, LANES), 0)
    for p in range(GROUP // 2):
        xs = jnp.concatenate([strided(x_scr, 2 * p + i, batch) for i in (0, 1)], axis=0).astype(BF)
        turn_scr[p] = jnp.dot(xs, mirror, preferred_element_type=F32).T.astype(BF)
        fall = jnp.exp(-rate_ref[p : p + 1, :] * away) * away
        got = jnp.dot(xs, fall.astype(BF), preferred_element_type=F32)
        h1_ref[p] = jnp.where(low_half, got[:batch], got[batch:])
    for p in range(GROUP // 2):
        ds = jnp.concatenate([strided(d_scr, 2 * p + i, batch) for i in (0, 1)], axis=0).astype(BF)
        for i in (0, 1):
            part = slice(i * batch, (i + 1) * batch)
            pairs = jnp.dot(turn_scr[p, :, part], ds[part], preferred_element_type=F32)
            pairs = jnp.where(col + row >= LANES - 1, pairs, 0.0)
            pairs = pltpu.roll(pairs, 1, 1, stride=1, stride_axis=0)
            lag_ref[2 * p + i : 2 * p + i + 1, :] = jnp.sum(pairs, axis=0, keepdims=True)
        grow = jnp.exp(-rate_ref[p : p + 1, :] * ahead)
        grow_scr[p, :, :LANES] = grow.astype(BF)
        grow1_low = (grow * ahead).astype(BF)
        grow_scr[p, :, LANES:] = grow1_low
        got = jnp.dot(ds, grow1_low, preferred_element_type=F32)
        g1_ref[p] = jnp.where(low_half, got[:batch], got[batch:])
    for p in range(GROUP // 2):
        lags = [lag_ref[2 * p + i : 2 * p + i + 1, :] for i in (0, 1)]
        high = [lag.astype(BF).astype(F32) for lag in lags]
        rest = jnp.where(lagrow == 2, lags[0] - high[0], lags[1] - high[1])
        stack = jnp.where(lagrow == 0, high[0], jnp.where(lagrow == 1, high[1], rest))
        stack = jnp.where(lagrow < 4, stack, 0.0).astype(BF)
        got = jnp.dot(stack, grow_scr[p], preferred_element_type=F32)
        even = got[0:1] + got[2:3]
        uneven = got[1:2] + got[3:4]
        s0_ref[p : p + 1, :] = jnp.where(low_row, even[:, :LANES], uneven[:, :LANES])
        s1_ref[p : p + 1, :] = jnp.where(low_row, even[:, LANES:], uneven[:, LANES:])


def bwd_post_kernel(
    dx_ref, gin_ref, coef_ref, rate_ref, k_ref, v_ref, tail_ref, taps_ref,
    dv_ref, ds_ref, head_ref, gtap_ref, out_ref,
):
    batch = k_ref.shape[0]
    taps = taps_ref.shape[1]
    away = (LANES - 1 - iota2(0)).astype(F32)
    low_half = lax.broadcasted_iota(jnp.int32, (batch, LANES), 1) < LANES // 2
    for p in range(GROUP // 2):
        decay = jnp.exp(-rate_ref[p : p + 1, :] * away).astype(BF)
        g = gin_ref[p] * coef_ref[p : p + 1, :]
        both = jnp.concatenate([jnp.where(low_half, g, 0.0), jnp.where(low_half, 0.0, g)], axis=0)
        cross = lax.dot_general(
            both.astype(BF), decay, (((1,), (1,)), ((), ())), preferred_element_type=F32
        )
        out_ref[pl.ds(2 * p, batch, stride=GROUP), :] = cross[:batch]
        out_ref[pl.ds(2 * p + 1, batch, stride=GROUP), :] = cross[batch:]
    lane = lax.broadcasted_iota(jnp.int32, (GROUP, LANES), 1)
    tail = tail_ref[...]
    spread = spread_taps(taps_ref)
    head = jnp.zeros((GROUP, LANES), F32)
    sums = [jnp.zeros((GROUP, LANES), F32) for _ in range(taps)]
    for b in range(batch):
        block = k_ref[b]
        edge = unpack_tail(tail, b, taps)
        lagged = [block] + [lag_rows(block, edge, i, lane) for i in range(1, taps)]
        shifted = spread[0] * block
        for i in range(1, taps):
            shifted = shifted + spread[i] * lagged[i]
        d_mixed = dx_ref[b] + out_ref[b * GROUP : (b + 1) * GROUP, :]
        dv_ref[b] = (d_mixed * shifted).astype(BF)
        d_shifted = d_mixed * v_ref[b]
        ds_ref[b] = d_shifted
        for i in range(taps):
            sums[i] = sums[i] + d_shifted * lagged[i]
        start = (taps - 1) * b
        head = jnp.where(
            (lane >= start) & (lane < start + taps - 1), pltpu.roll(d_shifted, start, 1), head
        )
    head_ref[...] = head
    packed = jnp.zeros((GROUP, LANES), F32)
    for i in range(taps):
        packed = jnp.where(lane == i, jnp.sum(sums[i], axis=1, keepdims=True), packed)
    gtap_ref[...] = packed


def first_kernel(
    at_ref, x_ref, cot_ref, gain_ref, wq_ref, wk_ref, wv_ref, normed_ref, cut_ref, q_ref, k_ref,
    v_ref, tail_ref, *, edge, chunks, parts
):
    step = pl.program_id(0)
    channels = wq_ref.shape[0]

    @pl.when(step == 0)
    def start():
        tail_ref[...] = jnp.zeros_like(tail_ref)

    seqs = x_ref.shape[0]
    rows = x_ref[...].reshape(seqs * LANES, x_ref.shape[2]).astype(F32)
    center = rows - jnp.mean(rows, axis=-1, keepdims=True)
    spread = jnp.mean(center * center, axis=-1, keepdims=True)
    normed = (center * lax.rsqrt(spread + 1e-05) * gain_ref[...]).astype(BF)
    normed_ref[...] = normed.reshape(normed_ref.shape)
    place = at_ref[1] * LANES + lax.broadcasted_iota(jnp.int32, cot_ref.shape[1:], 0)
    first = 2 + seqs * ((at_ref[0] ^ (step % parts)) * chunks + step // parts)
    for j in range(seqs):
        kept = jnp.where(place < at_ref[first + j], cot_ref[j].astype(F32), 0.0)
        cut_ref[j] = kept.astype(BF)
    lane = lax.broadcasted_iota(jnp.int32, (channels, LANES), 1)
    for w_ref, out_ref in ((wq_ref, q_ref), (wk_ref, k_ref), (wv_ref, v_ref)):
        out = lax.dot_general(
            w_ref[...], normed, (((1,), (1,)), ((), ())), preferred_element_type=F32
        )
        for j in range(seqs):
            block = out[:, j * LANES : (j + 1) * LANES]
            out_ref[j] = block
            if out_ref is k_ref:
                at = edge * (step * seqs + j)
                block = pltpu.roll(block, at + edge, 1)
                tail_ref[...] = jnp.where((lane >= at) & (lane < at + edge), block, tail_ref[...])


def last_kernel(
    dq_ref, dv_ref, ds_ref, spill_ref, taps_ref, normed_ref, wq_ref, wk_ref, wv_ref, *rest
):
    piece_refs = rest[:-2]
    grad_ref, gain_ref = rest[-2:]
    step = pl.program_id(0)
    seqs, channels, _ = dq_ref.shape
    taps = taps_ref.shape[1]
    edge = taps - 1

    @pl.when(step == 0)
    def start():
        grad_ref[...] = jnp.zeros_like(grad_ref)
        gain_ref[...] = jnp.zeros_like(gain_ref)

    lane = lax.broadcasted_iota(jnp.int32, (channels, LANES), 1)
    spread = spread_taps(taps_ref)
    sides = []
    for j in range(seqs):
        block = ds_ref[j]
        at = edge * (step * seqs + j)
        after = pltpu.roll(spill_ref[...], (LANES - at) % LANES, 1)
        d_keys = spread[0] * block
        for i in range(1, taps):
            moved = pltpu.roll(jnp.where(lane >= i, block, after), LANES - i, 1)
            d_keys = d_keys + spread[i] * moved
        sides.append(jnp.concatenate([dq_ref[j], d_keys.astype(BF), dv_ref[j]], axis=0))
    both = jnp.concatenate(sides, axis=1)
    normed = normed_ref[...].reshape(seqs * LANES, normed_ref.shape[2])
    grad_ref[: 2 * channels, :] += jnp.dot(both[channels:], normed, preferred_element_type=F32)
    weights = jnp.concatenate([wq_ref[...], wk_ref[...], wv_ref[...]], axis=0)
    rows = lax.dot_general(both, weights, (((0,), (0,)), ((), ())), preferred_element_type=F32)
    gain_ref[...] += jnp.sum(rows * normed.astype(F32), axis=0, keepdims=True)
    for i, piece_ref in enumerate(piece_refs):

        @pl.when(step == i)
        def store(piece_ref=piece_ref):
            piece_ref[...] = rows.reshape(piece_ref.shape)


def first_call(at, inputs, cotangent, gain, weights, edge, chunks, parts):
    num_seqs, _, width = inputs.shape
    channels = weights[0].shape[0]
    seqs = num_seqs // (chunks * parts)
    whole = pl.BlockSpec((channels, width), lambda s, m: (0, 0))
    act = pl.BlockSpec((seqs, channels, LANES), lambda s, m: (s, 0, 0))
    rows = pl.BlockSpec((seqs, LANES, width), lambda s, m: (s, 0, 0))
    a = shape(num_seqs, channels, LANES)
    own = pl.BlockSpec(
        (seqs, LANES, width),
        lambda s, m: ((m[0] ^ (s % parts)) * chunks + s // parts, 0, 0),
    )
    return pl.pallas_call(
        functools.partial(first_kernel, edge=edge, chunks=chunks, parts=parts),
        grid_spec=pltpu.PrefetchScalarGridSpec(
            num_scalar_prefetch=1,
            grid=(chunks * parts,),
            in_specs=[
                own,
                own,
                pl.BlockSpec((1, width), lambda s, m: (0, 0)),
                whole,
                whole,
                whole,
            ],
            out_specs=[
                rows,
                rows,
                act,
                act,
                act,
                pl.BlockSpec((channels, LANES), lambda s, m: (0, 0)),
            ],
        ),
        out_shape=[
            shape(num_seqs, LANES, width, dtype=BF),
            shape(num_seqs, LANES, width, dtype=BF),
            a,
            a,
            a,
            shape(channels, LANES),
        ],
    )(at, inputs, cotangent, gain[None, :], *weights)


def last_call(dq, dv, ds, spill, tap_rows, normed, weights, pieces, more):
    num_seqs, channels, _ = dq.shape
    taps = tap_rows.shape[1]
    width = normed.shape[2]
    seqs = num_seqs // pieces
    act = pl.BlockSpec((seqs, channels, LANES), lambda s: (s, 0, 0))
    out = pl.pallas_call(
        last_kernel,
        grid=(pieces,),
        in_specs=[
            act,
            act,
            act,
            pl.BlockSpec((channels, LANES), lambda s: (0, 0)),
            pl.BlockSpec((channels, taps), lambda s: (0, 0)),
            pl.BlockSpec((seqs, LANES, width), lambda s: (s, 0, 0)),
        ]
        + [pl.BlockSpec((channels, width), lambda s: (0, 0))] * 3,
        out_specs=[pl.BlockSpec((seqs, LANES, width), lambda s: (0, 0, 0))] * pieces
        + [
            pl.BlockSpec((2 * channels + more, width), lambda s: (0, 0)),
            pl.BlockSpec((1, width), lambda s: (0, 0)),
        ],
        out_shape=[shape(seqs, LANES, width)] * pieces
        + [shape(2 * channels + more, width), shape(1, width)],
    )(dq, dv, ds, spill, tap_rows, normed, *weights)
    return out[:-2], out[-2], out[-1]


def place_kernel(blocks_ref, *refs, count):
    step = pl.program_id(0)
    for i, piece_ref in enumerate(refs[:count]):

        @pl.when(step == i)
        def store(piece_ref=piece_ref):
            refs[-1][...] = piece_ref[...]


def place_call(blocks, pieces, rows, whole=None):
    count = len(pieces)
    piece = pieces[0].shape
    old = () if whole is None else (whole,)
    return pl.pallas_call(
        functools.partial(place_kernel, count=count),
        grid_spec=pltpu.PrefetchScalarGridSpec(
            num_scalar_prefetch=1,
            grid=(count,),
            in_specs=[pl.BlockSpec(piece, lambda s, b: (0, 0, 0))] * count
            + [pl.BlockSpec(memory_space=pl.ANY)] * len(old),
            out_specs=pl.BlockSpec(piece, lambda s, b: (b[s], 0, 0)),
        ),
        out_shape=shape(rows, *piece[1:]),
        input_output_aliases={count + 1: 0} if old else {},
    )(blocks, *pieces, *old)


def specs(batch, taps):
    return dict(
        act=pl.BlockSpec((batch, GROUP, LANES), lambda i: (0, i, 0)),
        row=pl.BlockSpec((GROUP, LANES), lambda i: (i, 0)),
        pair=pl.BlockSpec((GROUP // 2, LANES), lambda i: (i, 0)),
        state=pl.BlockSpec((GROUP // 2, batch, LANES), lambda i: (i, 0, 0)),
        taps=pl.BlockSpec((GROUP, taps), lambda i: (i, 0)),
        one=pl.BlockSpec((GROUP, 1), lambda i: (i, 0)),
    )


def shape(*dims, dtype=F32):
    return jax.ShapeDtypeStruct(dims, dtype)


def call(kernel, ins, outs, out_shapes, scratch, channels, args):
    return pl.pallas_call(
        kernel,
        grid=(channels // GROUP,),
        in_specs=ins,
        out_specs=outs,
        out_shape=out_shapes,
        scratch_shapes=scratch,
    )(*args)


def conv_calls(batch, channels, taps):
    s = specs(batch, taps)
    act, row, pair, state, tap, one = (s[n] for n in ("act", "row", "pair", "state", "taps", "one"))
    a = shape(batch, channels, LANES)
    alow = shape(batch, channels, LANES, dtype=BF)
    st = shape(channels // 2, batch, LANES)
    rows = shape(channels, LANES)
    pairs = shape(channels // 2, LANES)
    scr = pltpu.VMEM((batch * GROUP, LANES), F32)

    def fwd_local(k, v, tail, tap_rows, rate, kern):
        return call(fwd_local_kernel, [act, act, row, tap, pair, row], [act, act, state],
                    [a, a, st], [scr, scr], channels, (k, v, tail, tap_rows, rate, kern))

    def fwd_post(y, hin, coef, rate, mixed, q, skip):
        return call(fwd_post_kernel, [act, state, pair, pair, act, act, one],
                    [act, act], [a, alow], [scr], channels, (y, hin, coef, rate, mixed, q, skip))

    def bwd_local(dg, q, so, skip, rate, kern):
        return call(bwd_local_kernel, [act, act, act, one, pair, row],
                    [act, act, act, state], [alow, a, a, st], [scr, scr], channels,
                    (dg, q, so, skip, rate, kern))

    def bwd_lags(d, mixed, rate, part, parts):
        steps = channels // GROUP // parts
        ins = [
            pl.BlockSpec((batch, GROUP, LANES), lambda i: (0, i + part * steps, 0)),
            pl.BlockSpec((batch, GROUP, LANES), lambda i: (0, i + part * steps, 0)),
            pl.BlockSpec((GROUP // 2, LANES), lambda i: (i + part * steps, 0)),
        ]
        count = channels // parts
        sp = shape(count // 2, batch, LANES)
        two = shape(count // 2, LANES)
        return call(bwd_lags_kernel, ins, [state, state, row, pair, pair],
                    [sp, sp, shape(count, LANES), two, two],
                    [scr, scr, pltpu.VMEM((GROUP // 2, LANES, 2 * batch), BF),
                     pltpu.VMEM((GROUP // 2, LANES, 2 * LANES), BF)], count, (d, mixed, rate))

    def bwd_post(dx, gin, coef, rate, k, v, tail, tap_rows):
        return call(bwd_post_kernel, [act, state, pair, pair, act, act, row, tap],
                    [act, act, row, row], [alow, a, rows, rows], [scr], channels,
                    (dx, gin, coef, rate, k, v, tail, tap_rows))

    return fwd_local, fwd_post, bwd_local, bwd_lags, bwd_post


def passed_along(x, axis, by):
    count = lax.axis_size(axis)
    pairs = [(i, i + by) for i in range(count) if 0 <= i + by < count]
    return lax.ppermute(x, axis, pairs)


def swapped(x, axis, bit):
    return lax.ppermute(x, axis, [(i, i ^ bit) for i in range(lax.axis_size(axis))])


def summed(x, axes):
    for axis in axes:
        bit = 1
        while bit < lax.axis_size(axis):
            x = x + swapped(x, axis, bit)
            bit *= 2
    return x


def carried(own, decay, sign, fill=lambda got, step: got):
    count = lax.axis_size("seq")
    odd = lax.axis_index("seq") % 2 == 1
    rows = own.shape[0] // 2
    fall = jnp.where(odd, decay(1)[rows:], decay(1)[:rows])
    keep = jnp.where(odd, own[rows:], own[:rows])
    got = fill(swapped(jnp.where(odd, own[:rows], own[rows:]), "seq", 1), 0)
    leads = odd if sign < 0 else jnp.logical_not(odd)
    lead = jnp.where(leads, keep, got)
    both = fall * lead + jnp.where(leads, got, keep)
    into = fill(passed_along(both, "seq", 2 * sign), 1)
    reach = 1
    while reach < count // 2 - 1:
        far = jnp.where(odd, decay(2 * reach)[rows:], decay(2 * reach)[:rows])
        whole = both + fall * fall * into
        got = passed_along(whole, "seq", 2 * sign * (reach + 1))
        into = into + far * (fill(got, 2) if reach == 1 else got)
        reach = 2 * reach + 1
    then = fall * into + lead
    stay = jnp.where(leads, into, then)
    back = fill(swapped(jnp.where(leads, then, into), "seq", 1), 3)
    return jnp.concatenate([jnp.where(odd, back, stay), jnp.where(odd, stay, back)], axis=0)


class Link:
    def __init__(self):
        self.waits = ()
        self.last = ()

    def swap(self, x, *more, free=False):
        x, *_ = lax.optimization_barrier((x, *self.waits, *(() if free else self.last), *more))
        got = swapped(x, "tp", 2)
        self.waits = ()
        self.last = (got,)
        self.sent = x
        return got


def far_total(part):
    own, side = part if isinstance(part, (tuple, list)) else jnp.split(part, 2, axis=0)
    return own + swapped(side, "tp", 1)


def total_steps(x, digits):
    index = lax.axis_index("seq")
    for stride, radix in digits:
        digit = (index // stride) % radix
        rows = x.shape[0] // radix
        got = yield [
            (lax.dynamic_slice_in_dim(x, (digit ^ k) * rows, rows, 0), k * stride)
            for k in range(1, radix)
        ]
        x = sum(got, lax.dynamic_slice_in_dim(x, digit * rows, rows, 0))
    for stride, radix in reversed(digits):
        digit = (index // stride) % radix
        rows = x.shape[0]
        got = yield [(x, k * stride) for k in range(1, radix)]
        whole = jnp.zeros((radix * rows,) + x.shape[1:], x.dtype)
        for k, part in enumerate([x, *got]):
            whole = lax.dynamic_update_slice_in_dim(whole, part, (digit ^ k) * rows, 0)
        x = whole
    return x


class Total:
    def __init__(self, x):
        count = lax.axis_size("seq")
        digits = [(1, 2)]
        while digits[-1][0] * digits[-1][1] < count:
            stride = digits[-1][0] * digits[-1][1]
            digits.append((stride, min(4, count // stride)))
        self.rounds = 2 * len(digits)
        self.steps = total_steps(x, digits)
        self.sends = next(self.steps)

    def run(self, rounds, after=()):
        got = ()
        self.sends = [(lax.optimization_barrier((x, after))[0], by) for x, by in self.sends]
        for _ in range(rounds * self.rounds // 4):
            got = tuple(swapped(x, "seq", by) for x, by in self.sends)
            try:
                self.sends = self.steps.send(got)
            except StopIteration as end:
                self.done = end.value
        return got


def centered(rows):
    center = rows - jnp.mean(rows, axis=-1, keepdims=True)
    spread = jnp.mean(center * center, axis=-1, keepdims=True)
    inverse = lax.rsqrt(spread + 1e-05)
    return center * inverse, inverse


def norm_back(unit, inverse, grad, gain):
    scaled = grad * gain
    mean_one = jnp.mean(scaled, axis=-1, keepdims=True)
    mean_two = jnp.mean(scaled * unit, axis=-1, keepdims=True)
    return inverse * (scaled - mean_one - unit * mean_two)


def product(form, left, right):
    return jnp.einsum(form, left, right, preferred_element_type=F32)


def local(
    inputs,
    lengths,
    first_gain,
    query_weight,
    key_weight,
    value_weight,
    shift_taps,
    state_coef,
    state_rate,
    skip_gain,
    project_weight,
    second_gain,
    up_weight,
    down_weight,
    cotangent,
):
    place = lax.axis_index("seq")
    mine = lax.axis_index("tp")
    parts = lax.axis_size("tp")
    assert parts == 4
    num_seqs, block_len, width_all = inputs.shape
    taps = shift_taps.shape[0]
    channels, states = state_coef.shape
    assert block_len == LANES and 2 * states == LANES and channels % GROUP == 0
    edge = taps - 1
    chunks = 2
    size = num_seqs // chunks
    piece = size // parts
    half = 2 * piece
    group_seqs = num_seqs // parts

    def starts():
        for u in range(chunks):
            for r in range(parts):
                yield (mine ^ r) * group_seqs + u * piece

    def groups(x):
        return jnp.concatenate(
            [lax.dynamic_slice_in_dim(x, at, piece, 0) for at in starts()], axis=0
        )

    def placed(pieces, u, whole=None):
        blocks = jnp.stack([(mine ^ r) * chunks + u for r in range(parts)])
        return place_call(blocks, pieces, num_seqs, whole)

    own_inputs = [
        lax.dynamic_slice_in_dim(inputs, mine * group_seqs + u * piece, piece, 0).astype(F32)
        for u in range(chunks)
    ]

    def nears(x, u):
        return x[u * size : u * size + half]

    def fars(x, u):
        return x[u * size + half : (u + 1) * size]

    def owns(x, u):
        return x[u * size : u * size + piece]

    link = Link()
    ends = groups(lengths)
    positions = place * block_len + jnp.arange(block_len)
    valid = (positions[None, :] < ends[:, None])[:, :, None]
    fwd_local, fwd_post, bwd_local, bwd_lags, bwd_post = conv_calls(num_seqs, channels, taps)
    rate = state_rate.reshape(channels // 2, LANES)
    coef = state_coef.reshape(channels // 2, LANES)
    tap_rows = shift_taps.T
    skip = skip_gain[:, None]
    lag = jnp.arange(LANES).astype(F32)
    kern = jnp.sum(
        state_coef[:, :, None] * jnp.exp(-state_rate[:, :, None] * lag[None, None, :]), axis=1
    )

    def block_decay(count):
        return jnp.exp(-rate * (LANES * count))[:, None, :]

    turned = (query_weight.T, key_weight.T, value_weight.T)
    at = jnp.concatenate([jnp.stack([mine, place]), lengths])
    normed, d_mlp, queries, keys, values, tail = first_call(
        at, inputs, cotangent, first_gain, turned, edge, chunks, parts
    )
    tail = passed_along(tail, "seq", 1)
    conv, mixed, own = fwd_local(keys, values, tail, tap_rows, rate, kern)
    before = carried(own, block_decay, 1)
    state_out, gated_out = fwd_post(conv, before, coef, rate, mixed, queries, skip)

    sums = []
    for u in range(chunks):
        far = link.swap(far_total(product("bct,cd->btd", fars(gated_out, u), project_weight)))
        near = far_total(product("bct,cd->btd", nears(gated_out, u), project_weight))
        sums.append((near, far))
    def feed(first, d_out):
        up_act = product("btd,df->btf", first, up_weight)
        hidden, pull = jax.vjp(jax.nn.gelu, up_act)
        hidden = hidden.astype(BF)
        d_hidden = product("btd,fd->btf", d_out, down_weight)
        d_up = pull(d_hidden)[0].astype(BF)
        return hidden, d_up, product("btf,df->btd", d_up, up_weight)

    def scaled(*two):
        return (jnp.concatenate(two, axis=0) * second_gain).astype(BF)

    residuals = []
    units = []
    seconds = []
    fed = []
    for u in range(chunks):
        near, far = sums[u]
        residual = own_inputs[u] + (near + far)
        unit = centered(residual)
        residuals.append(residual)
        units.append(unit)
        side = swapped(unit[0], "tp", 1)
        far = link.swap(unit[0], free=u > 0)
        near_fed = feed(scaled(unit[0], side), nears(d_mlp, u))
        far, near_fed, fed = lax.optimization_barrier((far, near_fed, fed))
        second_far = scaled(far, swapped(far, "tp", 1))
        far_fed = feed(second_far, fars(d_mlp, u))
        seconds += [scaled(unit[0], side), second_far]
        fed += [near_fed, far_fed]
    hiddens = [x[0] for x in fed]
    d_ups = [x[1] for x in fed]
    sums = []
    for u in range(chunks):
        far = link.swap(far_total(fed[2 * u + 1][2]))
        if u == 0:
            late_mlp, late_up, _ = lax.optimization_barrier((d_mlp, d_ups, link.sent))
            grad_down = product("btf,btd->fd", jnp.concatenate(hiddens, axis=0), late_mlp)
            grad_up = product(
                "btd,btf->df", jnp.concatenate(seconds, axis=0), jnp.concatenate(late_up, axis=0)
            )
            early = jnp.concatenate([grad_up, grad_down], axis=0)
            far, early = lax.optimization_barrier((far, early))
            link.last = (far,)
        sums.append((far_total(fed[2 * u][2]), far))
    early = lax.psum_scatter(early, "seq", scatter_dimension=0, tiled=True)
    lowered = [product("btf,fd->btd", hidden, down_weight) for hidden in hiddens]
    grad_second = 0.0
    d_norms = []
    lows = []
    gated = []
    for u in range(chunks):
        d_second = sums[u][0] + sums[u][1]
        unit, inverse = units[u]
        d_norm = norm_back(unit, inverse, d_second, second_gain)
        grad_second = grad_second + jnp.sum(d_second * unit, axis=(0, 1))
        side = swapped(d_norm, "tp", 1)
        far = link.swap(d_norm)
        if u + 1 == chunks:
            far, lowered, lows, gated = lax.optimization_barrier((far, lowered, lows, gated))
        rows = jnp.concatenate([d_norm, side, far, swapped(far, "tp", 1)], axis=0)
        low = (rows + d_mlp[u * size : (u + 1) * size].astype(F32)).astype(BF)
        lows.append(low)
        gated.append(product("btd,cd->bct", low, project_weight))
        d_norms.append(d_norm)
    d_resid_low = jnp.concatenate(lows, axis=0)
    d_gated = jnp.concatenate(gated, axis=0)
    d_queries, d_state, d_part, back = bwd_local(
        d_gated, queries, state_out, skip, rate, kern[:, ::-1]
    )
    outs = []

    def lower(u, after):
        far = link.swap(far_total(lowered[2 * u + 1]), after)
        outs.append(far_total(lowered[2 * u]) + far)
        return far

    block_out = None

    def give_out(u, after):
        nonlocal block_out
        out = jnp.where(owns(valid, u), residuals[u] + outs[u], 0.0)
        side = swapped(out, "tp", 1)
        far = link.swap(out, after)
        block_out = placed([out, side, far, swapped(far, "tp", 1)], u, block_out)
        return far

    grad_project = product("bct,btd->cd", gated_out, d_resid_low)
    grad_query = product("bct,btd->cd", d_queries, normed)
    lagged = bwd_lags(d_state, mixed, rate, 0, 1)
    flying = lower(0, back)

    def back_fill(got, step):
        nonlocal lagged, grad_project, grad_query, early, flying
        if step == 1:
            got, grad_project, _ = lax.optimization_barrier((got, grad_project, flying))
            flying = lower(1, got)
        elif step == 2:
            got, lagged, early, _ = lax.optimization_barrier((got, lagged, early, flying))
            flying = give_out(0, got)
        elif step == 3:
            got, grad_query, _ = lax.optimization_barrier((got, grad_query, flying))
        return got

    after = carried(back, block_decay, -1, back_fill)
    early = lax.all_gather(early, "seq", axis=0, tiled=True)
    flying = give_out(1, after)
    others = Total(jnp.concatenate([grad_project, grad_query], axis=0))
    first_got = others.run(1, after)
    d_values, d_shifted, head, grad_taps = bwd_post(
        d_part, after, coef, rate, keys, values, tail, tap_rows
    )
    spill = passed_along(head, "seq", -1)
    spill, _ = lax.optimization_barrier((spill, (flying, first_got)))
    pieces, main, grad_first = last_call(
        d_queries, d_values, d_shifted, spill, tap_rows, normed, turned, chunks * parts, 64
    )
    own_lag, back_lag, lags, near, near_lag = lagged
    grow = jnp.exp(rate)
    grad_coef = jnp.sum(before * back, axis=1) + grow * near
    grad_rate = -coef * (
        jnp.sum(
            back_lag * before + after * (own_lag + LANES * block_decay(1) * before), axis=1
        )
        + grow * (near_lag - near)
    )
    pairs = channels // 2
    edges = jnp.concatenate([grad_taps[:, :taps].T.reshape(-1), lags[:, 0]])
    edges = jnp.pad(edges, (0, -edges.shape[0] % width_all)).reshape(-1, width_all)
    gains = jnp.concatenate([grad_first / first_gain, grad_second[None, :]])
    tables = [grad_coef.reshape(-1, width_all), grad_rate.reshape(-1, width_all), gains, edges]
    rows = sum(x.shape[0] for x in tables)
    tables.append(jnp.zeros((64 - rows, width_all), F32))
    main = lax.dynamic_update_slice(main, jnp.concatenate(tables, axis=0), (2 * channels, 0))
    mains = Total(main)
    rows = grad_up.shape[0]
    grad_up, grad_down = early[:rows], early[rows:]
    sums = []
    for u in range(chunks):
        at = parts * u
        far = link.swap(far_total((pieces[at + 2], pieces[at + 3])))
        link.waits += others.run(1, link.sent) + mains.run(1, link.sent) + ((block_out,) if u else ())
        sums.append((far_total((pieces[at], pieces[at + 1])), far))
    grad_inputs = None
    for u in range(chunks):
        d_first = sums[u][0] + sums[u][1]
        unit, inverse = centered(own_inputs[u])
        d_rows = d_norms[u] + owns(d_mlp, u).astype(F32)
        d_rows = d_rows + norm_back(unit, inverse, d_first, first_gain)
        side = swapped(d_rows, "tp", 1)
        far = link.swap(d_rows)
        link.waits += mains.run(1, link.sent)
        if u == 0:
            link.waits += (*others.run(1, link.sent), grad_up, grad_down)
        if u:
            far, grad_inputs = lax.optimization_barrier((far, grad_inputs))
        grad_inputs = placed([d_rows, side, far, swapped(far, "tp", 1)], u, grad_inputs)
    main = mains.done
    at = 2 * channels
    grad_key, grad_value = main[:channels].T, main[channels:at].T
    rows = pairs * LANES // width_all
    grad_coef = main[at : at + rows].reshape(channels, states)
    grad_rate = main[at + rows : at + 2 * rows].reshape(channels, states)
    at += 2 * rows
    gains = summed(main[at : at + 2], ("tp",))
    edges = main[at + 2 :].reshape(-1)
    grad_taps = edges[: taps * channels].reshape(taps, channels)
    grad_skip = edges[taps * channels : (taps + 1) * channels]
    grad_project, grad_query = others.done[:channels], others.done[channels:].T
    return (
        block_out,
        grad_inputs,
        gains[0],
        grad_query,
        grad_key,
        grad_value,
        grad_taps,
        grad_coef,
        grad_rate,
        grad_skip,
        grad_project,
        gains[1],
        grad_up,
        grad_down,
    )


def solution(mesh):
    return jax.shard_map(
        local,
        mesh=mesh,
        in_specs=(
            P(None, "seq", None),
            P(),
            P(),
            P(None, "tp"),
            P(None, "tp"),
            P(None, "tp"),
            P(None, "tp"),
            P("tp", None),
            P("tp", None),
            P("tp"),
            P("tp", None),
            P(),
            P(None, "tp"),
            P("tp", None),
            P(None, "seq", None),
        ),
        out_specs=(
            P(None, "seq", None),
            P(None, "seq", None),
            P(),
            P(None, "tp"),
            P(None, "tp"),
            P(None, "tp"),
            P(None, "tp"),
            P("tp", None),
            P("tp", None),
            P("tp"),
            P("tp", None),
            P(),
            P(None, "tp"),
            P("tp", None),
        ),
        check_vma=False,
    )
```

```python
import functools

import jax
import jax.numpy as jnp
from jax import lax
from jax.experimental import pallas as pl
from jax.experimental.pallas import tpu as pltpu
from jax.sharding import PartitionSpec as P

LANES = 128
GROUP = 64
BF = jnp.bfloat16
F32 = jnp.float32


def iota2(axis):
    return lax.broadcasted_iota(jnp.int32, (LANES, LANES), axis)


def strided(ref, c, rows):
    return ref[pl.ds(c, rows, stride=GROUP), :]


def lag_rows(block, edge, offset, lane):
    return pltpu.roll(jnp.where(lane < LANES - offset, block, edge), offset, 1)


def unpack_tail(tail, b, taps):
    return pltpu.roll(tail, (LANES - (taps - 1) * (b + 1)) % LANES, 1)


def spread_taps(taps_ref):
    rows, taps = taps_ref.shape
    return [jnp.broadcast_to(taps_ref[:, i : i + 1], (rows, LANES)) for i in range(taps)]


def shift_sum(block, tail, b, spread, lane):
    edge = unpack_tail(tail, b, len(spread))
    total = spread[0] * block
    for offset in range(1, len(spread)):
        total = total + spread[offset] * lag_rows(block, edge, offset, lane)
    return total


def fwd_local_kernel(
    k_ref, v_ref, tail_ref, taps_ref, rate_ref, kern_ref, y_ref, mixed_ref, h_ref, mix_ref, out_ref
):
    batch = k_ref.shape[0]
    lane = lax.broadcasted_iota(jnp.int32, (GROUP, LANES), 1)
    tail = tail_ref[...]
    spread = spread_taps(taps_ref)
    for b in range(batch):
        mixed = shift_sum(k_ref[b], tail, b, spread, lane) * v_ref[b]
        mix_ref[b * GROUP : (b + 1) * GROUP, :] = mixed
        mixed_ref[b] = mixed
    row = iota2(0)
    col = iota2(1)
    away = (LANES - 1 - row).astype(F32)
    low_half = lax.broadcasted_iota(jnp.int32, (batch, LANES), 1) < LANES // 2
    for p in range(GROUP // 2):
        xs = []
        for c in (2 * p, 2 * p + 1):
            x = strided(mix_ref, c, batch).astype(BF)
            xs.append(x)
            toep = jnp.broadcast_to(kern_ref[c : c + 1, :], (LANES, LANES))
            toep = pltpu.roll(toep, 0, 1, stride=1, stride_axis=0)
            toep = jnp.where(col >= row, toep, 0.0).astype(BF)
            out_ref[pl.ds(c, batch, stride=GROUP), :] = jnp.dot(
                x, toep, preferred_element_type=F32
            )
        decay = jnp.exp(-rate_ref[p : p + 1, :] * away)
        both = jnp.concatenate(xs, axis=0)
        grown = jnp.dot(both, decay.astype(BF), preferred_element_type=F32)
        h_ref[p] = jnp.where(low_half, grown[:batch], grown[batch:])
    for b in range(batch):
        y_ref[b] = out_ref[b * GROUP : (b + 1) * GROUP, :]


def fwd_post_kernel(
    y_ref, hin_ref, coef_ref, rate_ref, mixed_ref, q_ref, skip_ref, state_ref, gated_ref, out_ref
):
    batch = y_ref.shape[0]
    ahead = (iota2(0) + 1).astype(F32)
    low_half = lax.broadcasted_iota(jnp.int32, (batch, LANES), 1) < LANES // 2
    for p in range(GROUP // 2):
        grow = jnp.exp(-rate_ref[p : p + 1, :] * ahead).astype(BF)
        h = hin_ref[p] * coef_ref[p : p + 1, :]
        both = jnp.concatenate([jnp.where(low_half, h, 0.0), jnp.where(low_half, 0.0, h)], axis=0)
        cross = lax.dot_general(
            both.astype(BF), grow, (((1,), (1,)), ((), ())), preferred_element_type=F32
        )
        out_ref[pl.ds(2 * p, batch, stride=GROUP), :] = cross[:batch]
        out_ref[pl.ds(2 * p + 1, batch, stride=GROUP), :] = cross[batch:]
    skip = jnp.broadcast_to(skip_ref[...], (GROUP, LANES))
    for b in range(batch):
        state = y_ref[b] + out_ref[b * GROUP : (b + 1) * GROUP, :] + skip * mixed_ref[b]
        state_ref[b] = state
        gated_ref[b] = (q_ref[b] * state).astype(BF)


def bwd_local_kernel(
    dg_ref, q_ref, state_ref, skip_ref, rate_ref, kern_ref, dq_ref, d_ref, dx_ref, g_ref,
    d_scr, out_ref,
):
    batch = dg_ref.shape[0]
    for b in range(batch):
        dg = dg_ref[b]
        dq_ref[b] = (dg * state_ref[b]).astype(BF)
        d = dg * q_ref[b]
        d_ref[b] = d
        d_scr[b * GROUP : (b + 1) * GROUP, :] = d
    row = iota2(0)
    col = iota2(1)
    ahead = (row + 1).astype(F32)
    low_half = lax.broadcasted_iota(jnp.int32, (batch, LANES), 1) < LANES // 2
    for p in range(GROUP // 2):
        ds = []
        for c in (2 * p, 2 * p + 1):
            d = strided(d_scr, c, batch).astype(BF)
            ds.append(d)
            toep = jnp.broadcast_to(kern_ref[c : c + 1, :], (LANES, LANES))
            toep = pltpu.roll(toep, 1, 1, stride=1, stride_axis=0)
            toep = jnp.where(col <= row, toep, 0.0).astype(BF)
            out_ref[pl.ds(c, batch, stride=GROUP), :] = jnp.dot(
                d, toep, preferred_element_type=F32
            )
        grow = jnp.exp(-rate_ref[p : p + 1, :] * ahead)
        got = jnp.dot(jnp.concatenate(ds, axis=0), grow.astype(BF), preferred_element_type=F32)
        g_ref[p] = jnp.where(low_half, got[:batch], got[batch:])
    skip = jnp.broadcast_to(skip_ref[...], (GROUP, LANES))
    for b in range(batch):
        dx_ref[b] = out_ref[b * GROUP : (b + 1) * GROUP, :] + skip * d_ref[b]


def bwd_lags_kernel(
    d_ref, mixed_ref, rate_ref, h1_ref, g1_ref, lag_ref, s0_ref, s1_ref, x_scr, d_scr, turn_scr,
    grow_scr,
):
    batch = d_ref.shape[0]
    for b in range(batch):
        x_scr[b * GROUP : (b + 1) * GROUP, :] = mixed_ref[b]
        d_scr[b * GROUP : (b + 1) * GROUP, :] = d_ref[b]
    row = iota2(0)
    col = iota2(1)
    mirror = jnp.where(row + col == LANES - 1, 1.0, 0.0).astype(BF)
    ahead = (row + 1).astype(F32)
    away = (LANES - 1 - row).astype(F32)
    low_half = lax.broadcasted_iota(jnp.int32, (batch, LANES), 1) < LANES // 2
    low_row = lax.broadcasted_iota(jnp.int32, (1, LANES), 1) < LANES // 2
    lagrow = lax.broadcasted_iota(jnp.int32, (8, LANES), 0)
    for p in range(GROUP // 2):
        xs = jnp.concatenate([strided(x_scr, 2 * p + i, batch) for i in (0, 1)], axis=0).astype(BF)
        turn_scr[p] = jnp.dot(xs, mirror, preferred_element_type=F32).T.astype(BF)
        fall = jnp.exp(-rate_ref[p : p + 1, :] * away) * away
        got = jnp.dot(xs, fall.astype(BF), preferred_element_type=F32)
        h1_ref[p] = jnp.where(low_half, got[:batch], got[batch:])
    for p in range(GROUP // 2):
        ds = jnp.concatenate([strided(d_scr, 2 * p + i, batch) for i in (0, 1)], axis=0).astype(BF)
        for i in (0, 1):
            part = slice(i * batch, (i + 1) * batch)
            pairs = jnp.dot(turn_scr[p, :, part], ds[part], preferred_element_type=F32)
            pairs = jnp.where(col + row >= LANES - 1, pairs, 0.0)
            pairs = pltpu.roll(pairs, 1, 1, stride=1, stride_axis=0)
            lag_ref[2 * p + i : 2 * p + i + 1, :] = jnp.sum(pairs, axis=0, keepdims=True)
        grow = jnp.exp(-rate_ref[p : p + 1, :] * ahead)
        grow_scr[p, :, :LANES] = grow.astype(BF)
        grow1_low = (grow * ahead).astype(BF)
        grow_scr[p, :, LANES:] = grow1_low
        got = jnp.dot(ds, grow1_low, preferred_element_type=F32)
        g1_ref[p] = jnp.where(low_half, got[:batch], got[batch:])
    for p in range(GROUP // 2):
        lags = [lag_ref[2 * p + i : 2 * p + i + 1, :] for i in (0, 1)]
        high = [lag.astype(BF).astype(F32) for lag in lags]
        rest = jnp.where(lagrow == 2, lags[0] - high[0], lags[1] - high[1])
        stack = jnp.where(lagrow == 0, high[0], jnp.where(lagrow == 1, high[1], rest))
        stack = jnp.where(lagrow < 4, stack, 0.0).astype(BF)
        got = jnp.dot(stack, grow_scr[p], preferred_element_type=F32)
        even = got[0:1] + got[2:3]
        uneven = got[1:2] + got[3:4]
        s0_ref[p : p + 1, :] = jnp.where(low_row, even[:, :LANES], uneven[:, :LANES])
        s1_ref[p : p + 1, :] = jnp.where(low_row, even[:, LANES:], uneven[:, LANES:])


def bwd_post_kernel(
    dx_ref, gin_ref, coef_ref, rate_ref, k_ref, v_ref, tail_ref, taps_ref,
    dv_ref, ds_ref, head_ref, gtap_ref, out_ref,
):
    batch = k_ref.shape[0]
    taps = taps_ref.shape[1]
    away = (LANES - 1 - iota2(0)).astype(F32)
    low_half = lax.broadcasted_iota(jnp.int32, (batch, LANES), 1) < LANES // 2
    for p in range(GROUP // 2):
        decay = jnp.exp(-rate_ref[p : p + 1, :] * away).astype(BF)
        g = gin_ref[p] * coef_ref[p : p + 1, :]
        both = jnp.concatenate([jnp.where(low_half, g, 0.0), jnp.where(low_half, 0.0, g)], axis=0)
        cross = lax.dot_general(
            both.astype(BF), decay, (((1,), (1,)), ((), ())), preferred_element_type=F32
        )
        out_ref[pl.ds(2 * p, batch, stride=GROUP), :] = cross[:batch]
        out_ref[pl.ds(2 * p + 1, batch, stride=GROUP), :] = cross[batch:]
    lane = lax.broadcasted_iota(jnp.int32, (GROUP, LANES), 1)
    tail = tail_ref[...]
    spread = spread_taps(taps_ref)
    head = jnp.zeros((GROUP, LANES), F32)
    sums = [jnp.zeros((GROUP, LANES), F32) for _ in range(taps)]
    for b in range(batch):
        block = k_ref[b]
        edge = unpack_tail(tail, b, taps)
        lagged = [block] + [lag_rows(block, edge, i, lane) for i in range(1, taps)]
        shifted = spread[0] * block
        for i in range(1, taps):
            shifted = shifted + spread[i] * lagged[i]
        d_mixed = dx_ref[b] + out_ref[b * GROUP : (b + 1) * GROUP, :]
        dv_ref[b] = (d_mixed * shifted).astype(BF)
        d_shifted = d_mixed * v_ref[b]
        ds_ref[b] = d_shifted
        for i in range(taps):
            sums[i] = sums[i] + d_shifted * lagged[i]
        start = (taps - 1) * b
        head = jnp.where(
            (lane >= start) & (lane < start + taps - 1), pltpu.roll(d_shifted, start, 1), head
        )
    head_ref[...] = head
    packed = jnp.zeros((GROUP, LANES), F32)
    for i in range(taps):
        packed = jnp.where(lane == i, jnp.sum(sums[i], axis=1, keepdims=True), packed)
    gtap_ref[...] = packed


def first_kernel(
    at_ref, x_ref, cot_ref, gain_ref, wq_ref, wk_ref, wv_ref, normed_ref, cut_ref, q_ref, k_ref,
    v_ref, tail_ref, *, edge, chunks, parts
):
    step = pl.program_id(0)
    channels = wq_ref.shape[0]

    @pl.when(step == 0)
    def start():
        tail_ref[...] = jnp.zeros_like(tail_ref)

    seqs = x_ref.shape[0]
    rows = x_ref[...].reshape(seqs * LANES, x_ref.shape[2]).astype(F32)
    center = rows - jnp.mean(rows, axis=-1, keepdims=True)
    spread = jnp.mean(center * center, axis=-1, keepdims=True)
    normed = (center * lax.rsqrt(spread + 1e-05) * gain_ref[...]).astype(BF)
    normed_ref[...] = normed.reshape(normed_ref.shape)
    place = at_ref[1] * LANES + lax.broadcasted_iota(jnp.int32, cot_ref.shape[1:], 0)
    first = 2 + seqs * ((at_ref[0] ^ (step % parts)) * chunks + step // parts)
    for j in range(seqs):
        kept = jnp.where(place < at_ref[first + j], cot_ref[j].astype(F32), 0.0)
        cut_ref[j] = kept.astype(BF)
    lane = lax.broadcasted_iota(jnp.int32, (channels, LANES), 1)
    for w_ref, out_ref in ((wq_ref, q_ref), (wk_ref, k_ref), (wv_ref, v_ref)):
        out = lax.dot_general(
            w_ref[...], normed, (((1,), (1,)), ((), ())), preferred_element_type=F32
        )
        for j in range(seqs):
            block = out[:, j * LANES : (j + 1) * LANES]
            out_ref[j] = block
            if out_ref is k_ref:
                at = edge * (step * seqs + j)
                block = pltpu.roll(block, at + edge, 1)
                tail_ref[...] = jnp.where((lane >= at) & (lane < at + edge), block, tail_ref[...])


def last_kernel(
    dq_ref, dv_ref, ds_ref, spill_ref, taps_ref, normed_ref, wq_ref, wk_ref, wv_ref, *rest
):
    piece_refs = rest[:-2]
    grad_ref, gain_ref = rest[-2:]
    step = pl.program_id(0)
    seqs, channels, _ = dq_ref.shape
    taps = taps_ref.shape[1]
    edge = taps - 1

    @pl.when(step == 0)
    def start():
        grad_ref[...] = jnp.zeros_like(grad_ref)
        gain_ref[...] = jnp.zeros_like(gain_ref)

    lane = lax.broadcasted_iota(jnp.int32, (channels, LANES), 1)
    spread = spread_taps(taps_ref)
    sides = []
    for j in range(seqs):
        block = ds_ref[j]
        at = edge * (step * seqs + j)
        after = pltpu.roll(spill_ref[...], (LANES - at) % LANES, 1)
        d_keys = spread[0] * block
        for i in range(1, taps):
            moved = pltpu.roll(jnp.where(lane >= i, block, after), LANES - i, 1)
            d_keys = d_keys + spread[i] * moved
        sides.append(jnp.concatenate([dq_ref[j], d_keys.astype(BF), dv_ref[j]], axis=0))
    both = jnp.concatenate(sides, axis=1)
    normed = normed_ref[...].reshape(seqs * LANES, normed_ref.shape[2])
    grad_ref[: 2 * channels, :] += jnp.dot(both[channels:], normed, preferred_element_type=F32)
    weights = jnp.concatenate([wq_ref[...], wk_ref[...], wv_ref[...]], axis=0)
    rows = lax.dot_general(both, weights, (((0,), (0,)), ((), ())), preferred_element_type=F32)
    gain_ref[...] += jnp.sum(rows * normed.astype(F32), axis=0, keepdims=True)
    for i, piece_ref in enumerate(piece_refs):

        @pl.when(step == i)
        def store(piece_ref=piece_ref):
            piece_ref[...] = rows.reshape(piece_ref.shape)


def first_call(at, inputs, cotangent, gain, weights, edge, chunks, parts):
    num_seqs, _, width = inputs.shape
    channels = weights[0].shape[0]
    seqs = num_seqs // (chunks * parts)
    whole = pl.BlockSpec((channels, width), lambda s, m: (0, 0))
    act = pl.BlockSpec((seqs, channels, LANES), lambda s, m: (s, 0, 0))
    rows = pl.BlockSpec((seqs, LANES, width), lambda s, m: (s, 0, 0))
    a = shape(num_seqs, channels, LANES)
    own = pl.BlockSpec(
        (seqs, LANES, width),
        lambda s, m: ((m[0] ^ (s % parts)) * chunks + s // parts, 0, 0),
    )
    return pl.pallas_call(
        functools.partial(first_kernel, edge=edge, chunks=chunks, parts=parts),
        grid_spec=pltpu.PrefetchScalarGridSpec(
            num_scalar_prefetch=1,
            grid=(chunks * parts,),
            in_specs=[
                own,
                own,
                pl.BlockSpec((1, width), lambda s, m: (0, 0)),
                whole,
                whole,
                whole,
            ],
            out_specs=[
                rows,
                rows,
                act,
                act,
                act,
                pl.BlockSpec((channels, LANES), lambda s, m: (0, 0)),
            ],
        ),
        out_shape=[
            shape(num_seqs, LANES, width, dtype=BF),
            shape(num_seqs, LANES, width, dtype=BF),
            a,
            a,
            a,
            shape(channels, LANES),
        ],
    )(at, inputs, cotangent, gain[None, :], *weights)


def last_call(dq, dv, ds, spill, tap_rows, normed, weights, pieces, more):
    num_seqs, channels, _ = dq.shape
    taps = tap_rows.shape[1]
    width = normed.shape[2]
    seqs = num_seqs // pieces
    act = pl.BlockSpec((seqs, channels, LANES), lambda s: (s, 0, 0))
    out = pl.pallas_call(
        last_kernel,
        grid=(pieces,),
        in_specs=[
            act,
            act,
            act,
            pl.BlockSpec((channels, LANES), lambda s: (0, 0)),
            pl.BlockSpec((channels, taps), lambda s: (0, 0)),
            pl.BlockSpec((seqs, LANES, width), lambda s: (s, 0, 0)),
        ]
        + [pl.BlockSpec((channels, width), lambda s: (0, 0))] * 3,
        out_specs=[pl.BlockSpec((seqs, LANES, width), lambda s: (0, 0, 0))] * pieces
        + [
            pl.BlockSpec((2 * channels + more, width), lambda s: (0, 0)),
            pl.BlockSpec((1, width), lambda s: (0, 0)),
        ],
        out_shape=[shape(seqs, LANES, width)] * pieces
        + [shape(2 * channels + more, width), shape(1, width)],
    )(dq, dv, ds, spill, tap_rows, normed, *weights)
    return out[:-2], out[-2], out[-1]


def place_kernel(blocks_ref, *refs, count):
    step = pl.program_id(0)
    for i, piece_ref in enumerate(refs[:count]):

        @pl.when(step == i)
        def store(piece_ref=piece_ref):
            refs[-1][...] = piece_ref[...]


def place_call(blocks, pieces, rows, whole=None):
    count = len(pieces)
    piece = pieces[0].shape
    old = () if whole is None else (whole,)
    return pl.pallas_call(
        functools.partial(place_kernel, count=count),
        grid_spec=pltpu.PrefetchScalarGridSpec(
            num_scalar_prefetch=1,
            grid=(count,),
            in_specs=[pl.BlockSpec(piece, lambda s, b: (0, 0, 0))] * count
            + [pl.BlockSpec(memory_space=pl.ANY)] * len(old),
            out_specs=pl.BlockSpec(piece, lambda s, b: (b[s], 0, 0)),
        ),
        out_shape=shape(rows, *piece[1:]),
        input_output_aliases={count + 1: 0} if old else {},
    )(blocks, *pieces, *old)


def specs(batch, taps):
    return dict(
        act=pl.BlockSpec((batch, GROUP, LANES), lambda i: (0, i, 0)),
        row=pl.BlockSpec((GROUP, LANES), lambda i: (i, 0)),
        pair=pl.BlockSpec((GROUP // 2, LANES), lambda i: (i, 0)),
        state=pl.BlockSpec((GROUP // 2, batch, LANES), lambda i: (i, 0, 0)),
        taps=pl.BlockSpec((GROUP, taps), lambda i: (i, 0)),
        one=pl.BlockSpec((GROUP, 1), lambda i: (i, 0)),
    )


def shape(*dims, dtype=F32):
    return jax.ShapeDtypeStruct(dims, dtype)


def call(kernel, ins, outs, out_shapes, scratch, channels, args):
    return pl.pallas_call(
        kernel,
        grid=(channels // GROUP,),
        in_specs=ins,
        out_specs=outs,
        out_shape=out_shapes,
        scratch_shapes=scratch,
    )(*args)


def conv_calls(batch, channels, taps):
    s = specs(batch, taps)
    act, row, pair, state, tap, one = (s[n] for n in ("act", "row", "pair", "state", "taps", "one"))
    a = shape(batch, channels, LANES)
    alow = shape(batch, channels, LANES, dtype=BF)
    st = shape(channels // 2, batch, LANES)
    rows = shape(channels, LANES)
    pairs = shape(channels // 2, LANES)
    scr = pltpu.VMEM((batch * GROUP, LANES), F32)

    def fwd_local(k, v, tail, tap_rows, rate, kern):
        return call(fwd_local_kernel, [act, act, row, tap, pair, row], [act, act, state],
                    [a, a, st], [scr, scr], channels, (k, v, tail, tap_rows, rate, kern))

    def fwd_post(y, hin, coef, rate, mixed, q, skip):
        return call(fwd_post_kernel, [act, state, pair, pair, act, act, one],
                    [act, act], [a, alow], [scr], channels, (y, hin, coef, rate, mixed, q, skip))

    def bwd_local(dg, q, so, skip, rate, kern):
        return call(bwd_local_kernel, [act, act, act, one, pair, row],
                    [act, act, act, state], [alow, a, a, st], [scr, scr], channels,
                    (dg, q, so, skip, rate, kern))

    def bwd_lags(d, mixed, rate, part, parts):
        steps = channels // GROUP // parts
        ins = [
            pl.BlockSpec((batch, GROUP, LANES), lambda i: (0, i + part * steps, 0)),
            pl.BlockSpec((batch, GROUP, LANES), lambda i: (0, i + part * steps, 0)),
            pl.BlockSpec((GROUP // 2, LANES), lambda i: (i + part * steps, 0)),
        ]
        count = channels // parts
        sp = shape(count // 2, batch, LANES)
        two = shape(count // 2, LANES)
        return call(bwd_lags_kernel, ins, [state, state, row, pair, pair],
                    [sp, sp, shape(count, LANES), two, two],
                    [scr, scr, pltpu.VMEM((GROUP // 2, LANES, 2 * batch), BF),
                     pltpu.VMEM((GROUP // 2, LANES, 2 * LANES), BF)], count, (d, mixed, rate))

    def bwd_post(dx, gin, coef, rate, k, v, tail, tap_rows):
        return call(bwd_post_kernel, [act, state, pair, pair, act, act, row, tap],
                    [act, act, row, row], [alow, a, rows, rows], [scr], channels,
                    (dx, gin, coef, rate, k, v, tail, tap_rows))

    return fwd_local, fwd_post, bwd_local, bwd_lags, bwd_post


def passed_along(x, axis, by):
    count = lax.axis_size(axis)
    pairs = [(i, i + by) for i in range(count) if 0 <= i + by < count]
    return lax.ppermute(x, axis, pairs)


def swapped(x, axis, bit):
    return lax.ppermute(x, axis, [(i, i ^ bit) for i in range(lax.axis_size(axis))])


def summed(x, axes):
    for axis in axes:
        bit = 1
        while bit < lax.axis_size(axis):
            x = x + swapped(x, axis, bit)
            bit *= 2
    return x


def carried(own, decay, sign, fill=lambda got, step: got):
    count = lax.axis_size("seq")
    odd = lax.axis_index("seq") % 2 == 1
    rows = own.shape[0] // 2
    fall = jnp.where(odd, decay(1)[rows:], decay(1)[:rows])
    keep = jnp.where(odd, own[rows:], own[:rows])
    got = fill(swapped(jnp.where(odd, own[:rows], own[rows:]), "seq", 1), 0)
    leads = odd if sign < 0 else jnp.logical_not(odd)
    lead = jnp.where(leads, keep, got)
    both = fall * lead + jnp.where(leads, got, keep)
    into = fill(passed_along(both, "seq", 2 * sign), 1)
    reach = 1
    while reach < count // 2 - 1:
        far = jnp.where(odd, decay(2 * reach)[rows:], decay(2 * reach)[:rows])
        whole = both + fall * fall * into
        got = passed_along(whole, "seq", 2 * sign * (reach + 1))
        into = into + far * (fill(got, 2) if reach == 1 else got)
        reach = 2 * reach + 1
    then = fall * into + lead
    stay = jnp.where(leads, into, then)
    back = fill(swapped(jnp.where(leads, then, into), "seq", 1), 3)
    return jnp.concatenate([jnp.where(odd, back, stay), jnp.where(odd, stay, back)], axis=0)


class Link:
    def __init__(self):
        self.waits = ()
        self.last = ()

    def swap(self, x, *more, free=False):
        x, *_ = lax.optimization_barrier((x, *self.waits, *(() if free else self.last), *more))
        got = swapped(x, "tp", 2)
        self.waits = ()
        self.last = (got,)
        self.sent = x
        return got


def far_total(part):
    own, side = part if isinstance(part, (tuple, list)) else jnp.split(part, 2, axis=0)
    return own + swapped(side, "tp", 1)


def total_steps(x, digits):
    index = lax.axis_index("seq")
    for stride, radix in digits:
        digit = (index // stride) % radix
        rows = x.shape[0] // radix
        got = yield [
            (lax.dynamic_slice_in_dim(x, (digit ^ k) * rows, rows, 0), k * stride)
            for k in range(1, radix)
        ]
        x = sum(got, lax.dynamic_slice_in_dim(x, digit * rows, rows, 0))
    for stride, radix in reversed(digits):
        digit = (index // stride) % radix
        rows = x.shape[0]
        got = yield [(x, k * stride) for k in range(1, radix)]
        whole = jnp.zeros((radix * rows,) + x.shape[1:], x.dtype)
        for k, part in enumerate([x, *got]):
            whole = lax.dynamic_update_slice_in_dim(whole, part, (digit ^ k) * rows, 0)
        x = whole
    return x


class Total:
    def __init__(self, x):
        count = lax.axis_size("seq")
        digits = [(1, 2)]
        while digits[-1][0] * digits[-1][1] < count:
            stride = digits[-1][0] * digits[-1][1]
            digits.append((stride, min(4, count // stride)))
        self.rounds = 2 * len(digits)
        self.steps = total_steps(x, digits)
        self.sends = next(self.steps)

    def run(self, rounds, after=()):
        got = ()
        self.sends = [(lax.optimization_barrier((x, after))[0], by) for x, by in self.sends]
        for _ in range(rounds * self.rounds // 4):
            got = tuple(swapped(x, "seq", by) for x, by in self.sends)
            try:
                self.sends = self.steps.send(got)
            except StopIteration as end:
                self.done = end.value
        return got


def centered(rows):
    center = rows - jnp.mean(rows, axis=-1, keepdims=True)
    spread = jnp.mean(center * center, axis=-1, keepdims=True)
    inverse = lax.rsqrt(spread + 1e-05)
    return center * inverse, inverse


def norm_back(unit, inverse, grad, gain):
    scaled = grad * gain
    mean_one = jnp.mean(scaled, axis=-1, keepdims=True)
    mean_two = jnp.mean(scaled * unit, axis=-1, keepdims=True)
    return inverse * (scaled - mean_one - unit * mean_two)


def product(form, left, right):
    return jnp.einsum(form, left, right, preferred_element_type=F32)


def local(
    inputs,
    lengths,
    first_gain,
    query_weight,
    key_weight,
    value_weight,
    shift_taps,
    state_coef,
    state_rate,
    skip_gain,
    project_weight,
    second_gain,
    up_weight,
    down_weight,
    cotangent,
):
    place = lax.axis_index("seq")
    mine = lax.axis_index("tp")
    parts = lax.axis_size("tp")
    assert parts == 4
    num_seqs, block_len, width_all = inputs.shape
    taps = shift_taps.shape[0]
    channels, states = state_coef.shape
    assert block_len == LANES and 2 * states == LANES and channels % GROUP == 0
    edge = taps - 1
    chunks = 2
    size = num_seqs // chunks
    piece = size // parts
    half = 2 * piece
    group_seqs = num_seqs // parts

    def starts():
        for u in range(chunks):
            for r in range(parts):
                yield (mine ^ r) * group_seqs + u * piece

    def groups(x):
        return jnp.concatenate(
            [lax.dynamic_slice_in_dim(x, at, piece, 0) for at in starts()], axis=0
        )

    def placed(pieces, u, whole=None):
        blocks = jnp.stack([(mine ^ r) * chunks + u for r in range(parts)])
        return place_call(blocks, pieces, num_seqs, whole)

    own_inputs = [
        lax.dynamic_slice_in_dim(inputs, mine * group_seqs + u * piece, piece, 0).astype(F32)
        for u in range(chunks)
    ]

    def nears(x, u):
        return x[u * size : u * size + half]

    def fars(x, u):
        return x[u * size + half : (u + 1) * size]

    def owns(x, u):
        return x[u * size : u * size + piece]

    link = Link()
    ends = groups(lengths)
    positions = place * block_len + jnp.arange(block_len)
    valid = (positions[None, :] < ends[:, None])[:, :, None]
    fwd_local, fwd_post, bwd_local, bwd_lags, bwd_post = conv_calls(num_seqs, channels, taps)
    rate = state_rate.reshape(channels // 2, LANES)
    coef = state_coef.reshape(channels // 2, LANES)
    tap_rows = shift_taps.T
    skip = skip_gain[:, None]
    lag = jnp.arange(LANES).astype(F32)
    kern = jnp.sum(
        state_coef[:, :, None] * jnp.exp(-state_rate[:, :, None] * lag[None, None, :]), axis=1
    )

    def block_decay(count):
        return jnp.exp(-rate * (LANES * count))[:, None, :]

    turned = (query_weight.T, key_weight.T, value_weight.T)
    at = jnp.concatenate([jnp.stack([mine, place]), lengths])
    normed, d_mlp, queries, keys, values, tail = first_call(
        at, inputs, cotangent, first_gain, turned, edge, chunks, parts
    )
    tail = passed_along(tail, "seq", 1)
    conv, mixed, own = fwd_local(keys, values, tail, tap_rows, rate, kern)
    before = carried(own, block_decay, 1)
    state_out, gated_out = fwd_post(conv, before, coef, rate, mixed, queries, skip)

    sums = []
    for u in range(chunks):
        far = link.swap(far_total(product("bct,cd->btd", fars(gated_out, u), project_weight)))
        near = far_total(product("bct,cd->btd", nears(gated_out, u), project_weight))
        sums.append((near, far))
    def feed(first, d_out):
        up_act = product("btd,df->btf", first, up_weight)
        hidden, pull = jax.vjp(jax.nn.gelu, up_act)
        hidden = hidden.astype(BF)
        d_hidden = product("btd,fd->btf", d_out, down_weight)
        d_up = pull(d_hidden)[0].astype(BF)
        return hidden, d_up, [
            product("btf,df->btd", rows, up_weight) for rows in jnp.split(d_up, 2, axis=0)
        ]

    def scaled(*two):
        return (jnp.concatenate(two, axis=0) * second_gain).astype(BF)

    residuals = []
    units = []
    seconds = []
    fed = []
    for u in range(chunks):
        near, far = sums[u]
        residual = own_inputs[u] + (near + far)
        unit = centered(residual)
        residuals.append(residual)
        units.append(unit)
        side = swapped(unit[0], "tp", 1)
        far = link.swap(unit[0], free=u > 0)
        near_fed = feed(scaled(unit[0], side), nears(d_mlp, u))
        far, near_fed, fed = lax.optimization_barrier((far, near_fed, fed))
        second_far = scaled(far, swapped(far, "tp", 1))
        far_fed = feed(second_far, fars(d_mlp, u))
        seconds += [scaled(unit[0], side), second_far]
        fed += [near_fed, far_fed]
    hiddens = [x[0] for x in fed]
    d_ups = [x[1] for x in fed]
    sums = []
    for u in range(chunks):
        far = link.swap(far_total(fed[2 * u + 1][2]))
        if u == 0:
            late_mlp, late_up, _ = lax.optimization_barrier((d_mlp, d_ups, link.sent))
            grad_down = product("btf,btd->fd", jnp.concatenate(hiddens, axis=0), late_mlp)
            grad_up = product(
                "btd,btf->df", jnp.concatenate(seconds, axis=0), jnp.concatenate(late_up, axis=0)
            )
            early = jnp.concatenate([grad_up, grad_down], axis=0)
            far, early = lax.optimization_barrier((far, early))
            link.last = (far,)
        sums.append((far_total(fed[2 * u][2]), far))
    early = lax.psum_scatter(early, "seq", scatter_dimension=0, tiled=True)
    lowered = [
        [product("btf,fd->btd", rows, down_weight) for rows in jnp.split(hidden, 2, axis=0)]
        for hidden in hiddens
    ]
    grad_second = 0.0
    d_norms = []
    lows = []
    gated = []
    for u in range(chunks):
        d_second = sums[u][0] + sums[u][1]
        unit, inverse = units[u]
        d_norm = norm_back(unit, inverse, d_second, second_gain)
        grad_second = grad_second + jnp.sum(d_second * unit, axis=(0, 1))
        side = swapped(d_norm, "tp", 1)
        far = link.swap(d_norm)
        if u + 1 == chunks:
            far, lowered, lows, gated = lax.optimization_barrier((far, lowered, lows, gated))
        rows = jnp.concatenate([d_norm, side, far, swapped(far, "tp", 1)], axis=0)
        low = (rows + d_mlp[u * size : (u + 1) * size].astype(F32)).astype(BF)
        lows.append(low)
        gated.append(product("btd,cd->bct", low, project_weight))
        d_norms.append(d_norm)
    d_resid_low = jnp.concatenate(lows, axis=0)
    d_gated = jnp.concatenate(gated, axis=0)
    d_queries, d_state, d_part, back = bwd_local(
        d_gated, queries, state_out, skip, rate, kern[:, ::-1]
    )
    outs = []

    def lower(u, after):
        far = link.swap(far_total(lowered[2 * u + 1]), after)
        outs.append(far_total(lowered[2 * u]) + far)
        return far

    block_out = None

    def give_out(u, after):
        nonlocal block_out
        out = jnp.where(owns(valid, u), residuals[u] + outs[u], 0.0)
        side = swapped(out, "tp", 1)
        far = link.swap(out, after)
        block_out = placed([out, side, far, swapped(far, "tp", 1)], u, block_out)
        return far

    grad_project = product("bct,btd->cd", gated_out, d_resid_low)
    grad_query = product("bct,btd->cd", d_queries, normed)
    lagged = bwd_lags(d_state, mixed, rate, 0, 1)
    flying = lower(0, back)

    def back_fill(got, step):
        nonlocal lagged, grad_project, grad_query, early, flying
        if step == 1:
            got, grad_project, _ = lax.optimization_barrier((got, grad_project, flying))
            flying = lower(1, got)
        elif step == 2:
            got, lagged, early, _ = lax.optimization_barrier((got, lagged, early, flying))
            flying = give_out(0, got)
        elif step == 3:
            got, grad_query, _ = lax.optimization_barrier((got, grad_query, flying))
        return got

    after = carried(back, block_decay, -1, back_fill)
    early = lax.all_gather(early, "seq", axis=0, tiled=True)
    flying = give_out(1, after)
    others = Total(jnp.concatenate([grad_project, grad_query], axis=0))
    first_got = others.run(1, after)
    d_values, d_shifted, head, grad_taps = bwd_post(
        d_part, after, coef, rate, keys, values, tail, tap_rows
    )
    spill = passed_along(head, "seq", -1)
    spill, _ = lax.optimization_barrier((spill, (flying, first_got)))
    pieces, main, grad_first = last_call(
        d_queries, d_values, d_shifted, spill, tap_rows, normed, turned, chunks * parts, 64
    )
    own_lag, back_lag, lags, near, near_lag = lagged
    grow = jnp.exp(rate)
    grad_coef = jnp.sum(before * back, axis=1) + grow * near
    grad_rate = -coef * (
        jnp.sum(
            back_lag * before + after * (own_lag + LANES * block_decay(1) * before), axis=1
        )
        + grow * (near_lag - near)
    )
    pairs = channels // 2
    edges = jnp.concatenate([grad_taps[:, :taps].T.reshape(-1), lags[:, 0]])
    edges = jnp.pad(edges, (0, -edges.shape[0] % width_all)).reshape(-1, width_all)
    gains = jnp.concatenate([grad_first / first_gain, grad_second[None, :]])
    tables = [grad_coef.reshape(-1, width_all), grad_rate.reshape(-1, width_all), gains, edges]
    rows = sum(x.shape[0] for x in tables)
    tables.append(jnp.zeros((64 - rows, width_all), F32))
    main = lax.dynamic_update_slice(main, jnp.concatenate(tables, axis=0), (2 * channels, 0))
    mains = Total(main)
    rows = grad_up.shape[0]
    grad_up, grad_down = early[:rows], early[rows:]
    sums = []
    for u in range(chunks):
        at = parts * u
        far = link.swap(far_total((pieces[at + 2], pieces[at + 3])))
        link.waits += others.run(1, link.sent) + mains.run(1, link.sent) + ((block_out,) if u else ())
        sums.append((far_total((pieces[at], pieces[at + 1])), far))
    grad_inputs = None
    for u in range(chunks):
        d_first = sums[u][0] + sums[u][1]
        unit, inverse = centered(own_inputs[u])
        d_rows = d_norms[u] + owns(d_mlp, u).astype(F32)
        d_rows = d_rows + norm_back(unit, inverse, d_first, first_gain)
        side = swapped(d_rows, "tp", 1)
        far = link.swap(d_rows)
        link.waits += mains.run(1, link.sent)
        if u == 0:
            link.waits += (*others.run(1, link.sent), grad_up, grad_down)
        if u:
            far, grad_inputs = lax.optimization_barrier((far, grad_inputs))
        grad_inputs = placed([d_rows, side, far, swapped(far, "tp", 1)], u, grad_inputs)
    main = mains.done
    at = 2 * channels
    grad_key, grad_value = main[:channels].T, main[channels:at].T
    rows = pairs * LANES // width_all
    grad_coef = main[at : at + rows].reshape(channels, states)
    grad_rate = main[at + rows : at + 2 * rows].reshape(channels, states)
    at += 2 * rows
    gains = summed(main[at : at + 2], ("tp",))
    edges = main[at + 2 :].reshape(-1)
    grad_taps = edges[: taps * channels].reshape(taps, channels)
    grad_skip = edges[taps * channels : (taps + 1) * channels]
    grad_project, grad_query = others.done[:channels], others.done[channels:].T
    return (
        block_out,
        grad_inputs,
        gains[0],
        grad_query,
        grad_key,
        grad_value,
        grad_taps,
        grad_coef,
        grad_rate,
        grad_skip,
        grad_project,
        gains[1],
        grad_up,
        grad_down,
    )


def solution(mesh):
    return jax.shard_map(
        local,
        mesh=mesh,
        in_specs=(
            P(None, "seq", None),
            P(),
            P(),
            P(None, "tp"),
            P(None, "tp"),
            P(None, "tp"),
            P(None, "tp"),
            P("tp", None),
            P("tp", None),
            P("tp"),
            P("tp", None),
            P(),
            P(None, "tp"),
            P("tp", None),
            P(None, "seq", None),
        ),
        out_specs=(
            P(None, "seq", None),
            P(None, "seq", None),
            P(),
            P(None, "tp"),
            P(None, "tp"),
            P(None, "tp"),
            P(None, "tp"),
            P("tp", None),
            P("tp", None),
            P("tp"),
            P("tp", None),
            P(),
            P(None, "tp"),
            P("tp", None),
        ),
        check_vma=False,
    )
```
